32 devices in a mesh: rep: 2 (over x), node: 8 (over z, y), local: 2 (over core).
Axes of the slice: x: 2, y: 2, z: 4, core: 2. Of those that a mesh axis runs over, the one named last changes fastest.
Arguments:
- tokens: bfloat16 [2048, 7168], P(('rep', 'node', 'local')), parts along dimension 0, may hold values from -6 to 6
- gate_ids: int32 [2048, 4], P(('rep', 'node', 'local')), parts along dimension 0, may hold values from 0 to 7, all different within a row; in each aligned block of 64 rows (0 to 63, 64 to 127, ...) at most 64 rows name the same one
- gate_values: bfloat16 [2048, 4], P(('rep', 'node', 'local')), parts along dimension 0, may hold values from 0.049804688 to 1
- w_gate: bfloat16 [8, 7168, 1024], P('node', None, 'local'), may hold values from -0.0625 to 0.0625
- w_up: bfloat16 [8, 7168, 1024], P('node', None, 'local'), may hold values from -0.0625 to 0.0625
- w_down: bfloat16 [8, 1024, 7168], P('node', 'local'), may hold values from -0.1875 to 0.1875
Outputs:
- mixed: bfloat16 [2048, 7168], P(('rep', 'node', 'local')), parts along dimension 0
The draws below stay inside these ranges and needn't reach their ends.
There are 2 independent parts, one for each index of `rep`. The reference program is written for one: setup_inputs(seed, part) draws one part's arguments, and reference() takes and returns one part's arrays. A program takes and returns all parts, laid end to end along the dimension named above; an argument that names none is the same for every part. Nothing has to cross between parts.
Inputs may be any that keep to these rules, and one draw needn't show every extreme that they name: `gate_ids`: each row names 4 different experts. Within the rows of one device, no expert is named by more than 64 rows, and in every draw some expert is named by exactly 64 rows of some device.
All inputs are finite; a program needn't handle non-finite values.
Results may differ from the reference program's by a relative error of at most 0.0065.
Values may be sent and summed in bfloat16 or wider, within the bound.
A program may use at most 128 MiB of HBM per device.

```python
import math
import jax
import jax.numpy as jnp
import numpy as np
from jax import lax

D = 7168
HID = 1024
TOPK = 4
TOK_DEV = 64
EXPERTS = 8
CAP = 64
TOKENS = 1024
N_NODE = 8
N_LOCAL = 2


def block_levels(own_key, dims, shards, least, high):
    level, own = 1.0, jax.random.fold_in(own_key, 6)
    for axis_at, shards_of in shards:
        steps = jnp.exp(jax.random.uniform(jax.random.fold_in(own, axis_at), (shards_of,), jnp.float32, least / len(shards), high / len(shards)))
        level = level * jnp.repeat(steps, dims[axis_at] // shards_of).reshape([-1 if axis == axis_at else 1 for axis in range(len(dims))])
    return level


def shared_out(own_key, own, number, rows, amount, top, limit, lean):
    order = jax.random.permutation(own_key, amount)
    crowded, common = shares(amount, rows * top, limit, lean, True), shares(amount, rows * top, limit, lean, False)
    places = jnp.arange(amount)

    def named(tallies, rotation):
        used = int((tallies > 0).sum())
        fixed = max(1, used // 4)
        moved = fixed + (places - fixed + rotation * (used - fixed)) % max(1, amount - fixed)
        return jnp.zeros((amount,), jnp.int32).at[order[jnp.where(places < fixed, places, moved)]].set(jnp.asarray(tallies, jnp.int32))

    tallies = jnp.where(number % 4 == 0, named(crowded, number // 4), named(common, number - number // 4 - 1))
    mixed = jax.random.permutation(jax.random.fold_in(own, 3), amount)
    source_of, receiver = mixed[0:amount // 2 * 2:2], mixed[1:amount // 2 * 2:2]
    slack = jnp.minimum(tallies[source_of] - 1, limit - tallies[receiver]) // 2
    slack = jnp.where((source_of == order[0]) | (receiver == order[0]) | (tallies[receiver] == 0), 0, jnp.maximum(slack, 0))
    moved = jax.random.randint(jax.random.fold_in(own, 4), (amount // 2,), 0, 1 << 20) % (slack + 1)
    tallies = tallies.at[source_of].add(-moved).at[receiver].add(moved)
    members = jnp.searchsorted(jnp.cumsum(tallies), jnp.arange(rows * top), side="right").astype(jnp.int32)
    listing = members.reshape(top, rows).T
    listing = listing[jax.random.permutation(jax.random.fold_in(own, 1), rows)]
    rotation = jax.random.randint(jax.random.fold_in(own, 2), (rows, 1), 0, top)
    return jnp.take_along_axis(listing, (jnp.arange(top)[None, :] + rotation) % top, axis=1)


def shares(number_of, total, reach, slope, full):
    weights = [(1 << 20) // math.isqrt(grade ** slope) + 1 for grade in range(1, number_of + 1)]
    largest = reach if full else min(reach, max(-(-total // number_of), total * weights[0] // sum(weights)))
    least = 1 if total - largest >= number_of - 1 else 0
    given, surplus = [largest] + [least] * (number_of - 1), total - largest - least * (number_of - 1)
    while surplus > 0:
        movable = [i for i in range(1, number_of) if given[i] < largest] or [i for i in range(1, number_of) if given[i] < reach]
        pool, left = sum([weights[i] for i in movable]), surplus
        for i in movable:
            addition = min(reach - given[i], max(1, left * weights[i] // pool), surplus)
            given[i] = given[i] + addition
            surplus = surplus - addition
    return np.array(given)


def normal_values(own_key, shape, scale, reach, shards=(), kind=jnp.bfloat16):
    factor_of = block_levels(own_key, shape, shards, -0.22, 0.18) if shards else 1.0
    array = jax.random.normal(own_key, shape, jnp.float32) * scale * factor_of
    return jnp.minimum(jnp.maximum(array, -reach), reach).astype(kind)


def setup_inputs(seed: int = 0, part: int = 0) -> dict:
    splits = jax.random.split(jax.random.key(seed), 7)
    part_splits = jax.random.split(jax.random.fold_in(splits[6], part), 7)
    tokens = normal_values(part_splits[0], (TOKENS, D), 1.0, 6.0, ((0, 16),))
    gate_ids_keys = jax.random.split(jax.random.fold_in(part_splits[1], 1), TOKENS // TOK_DEV)
    gate_ids_turns = jax.random.permutation(jax.random.fold_in(part_splits[1], 3), TOKENS // TOK_DEV)
    gate_ids = jax.vmap(lambda own, number: shared_out(jax.random.fold_in(part_splits[1], 2), own, number, TOK_DEV, EXPERTS, TOPK, CAP, 2))(gate_ids_keys, gate_ids_turns).reshape((TOKENS, TOPK))
    gate_values = jnp.clip(jnp.exp(math.log(1.0) - 2.9996462 * jax.random.uniform(part_splits[2], (TOKENS, TOPK), jnp.float32) ** block_levels(part_splits[2], (TOKENS, TOPK), ((0, 16),), -0.2, 0.2)), 0.049804688, 1.0).astype(jnp.bfloat16)
    w_gate = normal_values(splits[3], (EXPERTS, D, HID), D ** -0.5, 0.0625, ((0, 8), (2, 2)))
    w_up = normal_values(splits[4], (EXPERTS, D, HID), D ** -0.5, 0.0625, ((0, 8), (2, 2)))
    w_down = normal_values(splits[5], (EXPERTS, HID, D), HID ** -0.5, 0.1875, ((0, 8), (1, 2)))
    return {"tokens": tokens, "gate_ids": gate_ids, "gate_values": gate_values, "w_gate": w_gate, "w_up": w_up, "w_down": w_down}


def slot_tables(gate_ids, gate_values):
    flat_ids = gate_ids.reshape(-1).astype(jnp.int32)
    expert_row = jnp.arange(EXPERTS, dtype=jnp.int32)
    onehot = (flat_ids[:, None] == expert_row[None, :]).astype(jnp.int32)
    earlier = jnp.cumsum(onehot, axis=0) - onehot
    within = jnp.sum(earlier * onehot, axis=1).astype(jnp.int32)
    slot = (flat_ids * CAP + within).reshape(TOK_DEV, TOPK)
    slot_row = jnp.arange(EXPERTS * CAP, dtype=jnp.int32)
    matches = slot[:, :, None] == slot_row[None, None, :]
    select = jnp.any(matches, axis=1).astype(jnp.bfloat16)
    combine_table = jnp.sum(jnp.where(matches, gate_values.astype(jnp.float32)[:, :, None], jnp.float32(0.0)), axis=1).astype(jnp.bfloat16)
    return select, combine_table


def expert_rows(args):
    rows, gate_mat, up_mat, down_mat = args
    gate_act = jnp.dot(rows, gate_mat, preferred_element_type=jnp.float32)
    up_act = jnp.dot(rows, up_mat, preferred_element_type=jnp.float32)
    hidden = (jax.nn.silu(gate_act) * up_act).astype(jnp.bfloat16)
    group = HID // N_LOCAL
    summed = jnp.zeros((rows.shape[0], D), jnp.float32)
    for part_index in range(N_LOCAL):
        piece = jnp.dot(hidden[:, part_index * group:(part_index + 1) * group], down_mat[part_index * group:(part_index + 1) * group], preferred_element_type=jnp.float32).astype(jnp.bfloat16)
        piece = lax.optimization_barrier(piece)
        summed = summed + piece.astype(jnp.float32)
    return summed.astype(jnp.bfloat16)


def reference(tokens, gate_ids, gate_values, w_gate, w_up, w_down):
    devices = N_NODE * N_LOCAL
    token_blocks = tokens.reshape(devices, TOK_DEV, D)
    select, combine_table = jax.vmap(slot_tables)(gate_ids.reshape(devices, TOK_DEV, TOPK), gate_values.reshape(devices, TOK_DEV, TOPK))
    dispatched = jnp.einsum("nts,ntd->nsd", select.astype(jnp.float32), token_blocks.astype(jnp.float32), precision=lax.Precision.HIGHEST).astype(jnp.bfloat16)
    by_expert = dispatched.reshape(devices, EXPERTS, CAP, D).transpose(1, 0, 2, 3).reshape(EXPERTS, devices * CAP, D)
    expert_out = lax.map(expert_rows, (by_expert, w_gate, w_up, w_down))
    back = expert_out.reshape(EXPERTS, devices, CAP, D).transpose(1, 0, 2, 3).reshape(devices, EXPERTS * CAP, D)
    mixed = jnp.einsum("nts,nsd->ntd", combine_table.astype(jnp.float32), back.astype(jnp.float32), precision=lax.Precision.HIGHEST)
    return mixed.astype(jnp.bfloat16).reshape(TOKENS, D)
```

```python
import functools

import jax
import jax.numpy as jnp
from jax import lax
from jax.experimental import pallas as pl
from jax.experimental.pallas import tpu as pltpu
from jax.sharding import PartitionSpec as P

MESH = pl.DeviceIdType.MESH
LANES = 128
VMEM_LIMIT = 67_000_000
PLANES = 4
COLUMNS = 2
SLICES = 2
SINGLE = (34, 56)

SCHEDULE = (
    (
        (("yA", 0, 0), ("yB", 0, 0), ("zA", 0, 1, 1), ("zA", 0, 0, 1), ("wyA", 0, 0), ("yB", 0, 1), ("wzA", 1, 0), ("wyB", 0, 0), ("zB", 0, 0, 1), ("yA", 1, 0), ("wzB", 1, 0), ("pa", 1, 0, 0), ("wyA", 1, 0), ("pa", 1, 0, 1), ("wyB", 0, 1), ("yA", 0, 1), ("pa", 0, 0, 0), ("zB", 0, 1, 1), ("pa", 0, 0, 1), ("C", 1, 0),),
        (("wzA", 2, 0), ("yA", 2, 0), ("C", 0, 0),),
        (("S", 1, 0), ("TB", 1, 0), ("yr", 1, 0), ("wzB", 2, 0), ("pa", 2, 0, 0), ("wyA", 2, 0), ("pa", 2, 0, 1), ("wyA", 0, 1), ("C", 2, 0),),
        (("wzA", 3, 0), ("yA", 3, 0), ("pa", 0, 1, 1), ("pa", 0, 1, 0), ("S", 2, 0), ("yr", 2, 0), ("TA", 1, 0), ("TB", 2, 0), ("wyA", 3, 0), ("wzB", 3, 0), ("S", 0, 0), ("wzA", 1, 1), ("pa", 3, 0, 0), ("yr", 0, 0), ("pa", 3, 0, 1), ("C", 0, 1),),
        (("wzA", 3, 1), ("TA", 2, 0), ("yA", 3, 1), ("C", 3, 0),),
        (("S", 0, 1), ("S", 3, 0), ("TB", 3, 0), ("wzA", 2, 1), ("yr", 3, 0), ("yA", 2, 1), ("wyA", 3, 1), ("wzB", 3, 1), ("pa", 3, 1, 0), ("pa", 3, 1, 1), ("C", 3, 1),),
        (("TA", 3, 0), ("yA", 1, 1), ("wzB", 2, 1), ("pa", 2, 1, 0), ("S", 3, 1), ("wyA", 2, 1), ("TB", 3, 1), ("pa", 2, 1, 1), ("C", 2, 1),),
        (("wzB", 1, 1), ("yr", 3, 1), ("pa", 1, 1, 0), ("wyA", 1, 1), ("S", 2, 1), ("TB", 2, 1), ("yr", 2, 1), ("TA", 3, 1), ("yr", 0, 1), ("pa", 1, 1, 1), ("C", 1, 1),),
        (("TA", 2, 1), ("FB1", 0, 0), ("S", 1, 1), ("TB", 1, 1), ("yr", 1, 1), ("TA", 1, 1), ("FB1", 0, 1), ("FB0", 0, 1), ("FA", 0, 0), ("FA", 0, 1), ("FB0", 0, 0),),
    ),
    (
        (("zA", 1, 0, -1), ("yB", 1, 0), ("zA", 1, 0, 1), ("yB", 1, 1), ("zA", 1, 1, 1), ("pa", 1, 0, 0), ("wyB", 1, 0), ("yA", 1, 0), ("zB", 1, 0, -1), ("zB", 1, 0, 1), ("wzA", 2, 0), ("wzA", 0, 0), ("wyB", 1, 1), ("yA", 2, 0), ("zA", 1, 1, -1), ("pa", 1, 1, 0), ("zA", 2, 0, -1), ("wzB", 2, 0), ("wzA", 0, 1), ("zA", 0, 0, 1), ("wyA", 2, 0), ("yA", 0, 1), ("wzB", 0, 0), ("wyA", 1, 0), ("pa", 0, 0, 0), ("pa", 1, 0, 1), ("yA", 1, 1), ("yA", 0, 0), ("zB", 0, 0, 1), ("zB", 2, 0, -1), ("wzA", 3, 0), ("zA", 3, 0, -1), ("C", 1, 0),),
        (("pa", 2, 0, 1), ("pa", 2, 0, 0), ("zA", 0, 1, 1), ("wzA", 2, 1), ("yA", 3, 0), ("wzB", 3, 0), ("zB", 1, 1, 1), ("zB", 3, 0, -1), ("C", 2, 0),),
        (("S", 1, 0), ("wyA", 3, 0), ("wzB", 0, 1), ("wzA", 3, 1), ("wyA", 1, 1), ("zA", 3, 1, -1), ("wyA", 0, 0), ("pa", 0, 0, 1), ("zA", 2, 1, -1), ("yA", 2, 1), ("pa", 3, 0, 1), ("zB", 0, 1, 1), ("wzB", 2, 1), ("wyA", 0, 1), ("C", 0, 0),),
        (("S", 2, 0), ("wyA", 2, 1), ("pa", 2, 1, 1), ("pa", 2, 1, 0), ("wzB", 3, 1), ("zB", 3, 1, -1), ("yA", 3, 1), ("pa", 3, 0, 0), ("yr", 2, 0), ("pa", 0, 1, 1), ("C", 3, 0),),
        (("zB", 2, 1, -1), ("TB", 2, 0), ("pa", 1, 1, 1), ("S", 0, 0), ("pa", 0, 1, 0), ("yr", 0, 0), ("pa", 3, 1, 0), ("C", 2, 1),),
        (("S", 3, 0), ("TA", 2, 0), ("TB", 3, 0), ("zB", 1, 1, -1), ("wyA", 3, 1), ("pa", 3, 1, 1), ("yr", 3, 0), ("S", 2, 1), ("C", 3, 1),),
        (("FB1", 1, 0), ("TA", 3, 0), ("yr", 1, 0), ("C", 1, 1),),
        (("S", 3, 1), ("TB", 3, 1), ("TB", 0, 0), ("yr", 3, 1), ("C", 0, 1),),
        (("TB", 2, 1), ("S", 0, 1), ("yr", 2, 1), ("TB", 0, 1), ("yr", 0, 1), ("TA", 0, 0), ("S", 1, 1), ("TA", 3, 1), ("yr", 1, 1), ("FA", 1, 0), ("TA", 2, 1), ("TA", 0, 1), ("FB0", 1, 0), ("FB1", 1, 1), ("FA", 1, 1), ("FB0", 1, 1),),
    ),
)


def chunk_of(size, most=1024):
    chunk = most
    while size % chunk:
        chunk -= LANES
    return chunk


def expert_weights(gate_ids, gate_values, columns):
    expert_row = jnp.arange(columns, dtype=jnp.int32)
    return jnp.sum(
        jnp.where(
            gate_ids[:, :, None] == expert_row[None, None, :],
            gate_values.astype(jnp.float32)[:, :, None],
            jnp.float32(0.0),
        ),
        axis=1,
    ).astype(jnp.bfloat16)


def single_columns(width):
    return max(LANES, width * SINGLE[0] // (SINGLE[1] * LANES) * LANES)


def tree_kernel(
    tokens, ids, values, wg_hbm, wu_hbm, wd_hbm, out,
    x, wg, wu, wd, pin, pout, own, rs_a, rs_b, yr_a, yr_b,
    weight_sem, own_sem, za_send, za_recv, zb_send, zb_recv, ya_send, ya_recv, yb_send, yb_recv,
    pa_send, pa_recv, pp_send, pp_recv, ra_send, ra_recv, rb_send, rb_recv,
    yra_send, yra_recv, yrb_send, yrb_recv,
):
    tok, width = tokens.shape
    wa = single_columns(width)
    rows = tok // SLICES
    node = lax.axis_index("node")
    other_core = {"local": 1 - lax.axis_index("local")}
    plane, column = node // COLUMNS, node % COLUMNS
    across = {"node": node + 1 - 2 * column}
    flip = jnp.where(plane >= PLANES // 2, 1, 0)
    near = plane * (1 - flip) + (PLANES - 1 - plane) * flip

    def actual(t):
        return t * (1 - flip) + (PLANES - 1 - t) * flip

    def along(s):
        return {"node": node + COLUMNS * s * (1 - 2 * flip)}

    def upward(s):
        return (1 - flip) if s > 0 else flip

    cols_a, cols_b, cols_bt = pl.ds(0, wa), pl.ds(wa, width - wa), pl.ds(wa, width + LANES - wa)

    keeps = [
        pltpu.make_async_copy(
            tokens.at[pl.ds(h * rows, rows)],
            x.at[plane, h, pl.ds(0, rows), pl.ds(0, width)],
            own_sem.at[h],
        )
        for h in range(SLICES)
    ]
    for keep in keeps:
        keep.start()
    loads = [
        pltpu.make_async_copy(src, dst, weight_sem.at[k])
        for k, (src, dst) in enumerate(((wg_hbm, wg), (wu_hbm, wu), (wd_hbm, wd)))
    ]

    barrier = pltpu.get_barrier_semaphore()
    for target in (other_core, across, along(1)):
        pl.semaphore_signal(barrier, inc=1, device_id=target, device_id_type=MESH)

    @pl.when(near > 0)
    def _():
        pl.semaphore_signal(barrier, inc=1, device_id=along(-1), device_id_type=MESH)

    table_row = lax.broadcasted_iota(jnp.int32, (LANES, tok), 0)
    turned = jnp.zeros((LANES, tok), jnp.float32)
    for choice in range(ids.shape[0]):
        chosen = table_row == ids[pl.ds(choice, 1), :]
        turned += jnp.where(chosen, values[pl.ds(choice, 1), :].astype(jnp.float32), 0.0)
    ones = lax.broadcasted_iota(jnp.int32, (tok, tok), 0) == lax.broadcasted_iota(
        jnp.int32, (tok, tok), 1
    )
    table = lax.dot_general(
        jnp.where(ones, 1.0, 0.0).astype(jnp.bfloat16), turned.astype(jnp.bfloat16),
        (((1,), (1,)), ((), ())), preferred_element_type=jnp.float32,
    ).astype(jnp.bfloat16)
    for h in range(SLICES):
        x[plane, h, pl.ds(0, rows), pl.ds(width, LANES)] = table[h * rows:(h + 1) * rows]
    for keep in keeps:
        keep.wait()
    for load in loads:
        load.start()
    pl.semaphore_wait(barrier, 3 + jnp.where(near > 0, 1, 0))

    first, second, both = pl.ds(0, rows), pl.ds(rows, rows), pl.ds(0, 2 * rows)

    def copy(src, dst, send, recv, target):
        return pltpu.make_async_remote_copy(
            src_ref=src, dst_ref=dst, send_sem=send, recv_sem=recv,
            device_id=target, device_id_type=MESH,
        )

    def sums(t, s):
        up = upward(s)
        return up, actual(t) - up

    def send(op):
        kind, t, h = op[:3]
        p = actual(t)
        if kind == "zA":
            ref = x.at[p, h, first, cols_a]
            return copy(ref, ref, za_send.at[max(op[3], 0), p, h], za_recv.at[p, h], along(op[3]))
        if kind == "zB":
            ref = x.at[p, h, both, cols_bt]
            return copy(ref, ref, zb_send.at[max(op[3], 0), p, h], zb_recv.at[p, h], along(op[3]))
        if kind == "yA":
            return copy(
                x.at[p, h, first, cols_a], x.at[p, h, second, cols_a],
                ya_send.at[p, h], ya_recv.at[p, h], across,
            )
        if kind == "yB":
            return copy(
                x.at[p, h, first, cols_bt], x.at[p, h, second, cols_bt],
                yb_send.at[h], yb_recv.at[h], across,
            )
        if kind == "pa":
            return copy(
                x.at[p, h, pl.ds(op[3] * rows, rows)], x.at[p, h, pl.ds((2 + op[3]) * rows, rows)],
                pa_send.at[p, h, op[3]], pa_recv.at[p, h, op[3]], other_core,
            )
        if kind == "yr":
            return copy(
                pin.at[p, h, second, cols_a], yr_a.at[p, h],
                yra_send.at[p, h], yra_recv.at[p, h], across,
            )
        if kind == "FB1":
            return copy(
                pin.at[p, h, second, cols_b], yr_b.at[h], yrb_send.at[h], yrb_recv.at[h], across
            )
        up, place = sums(t, op[3])
        if kind == "TA":
            return copy(
                pin.at[p, h, first, cols_a], rs_a.at[up, place, h],
                ra_send.at[p, h], ra_recv.at[up, p, h], along(op[3]),
            )
        return copy(
            pin.at[p, h, both, cols_b], rs_b.at[up, place, h],
            rb_send.at[p, h], rb_recv.at[up, p, h], along(op[3]),
        )

    def pp(p, h, slot):
        return copy(pout.at[slot], pin.at[p, h], pp_send.at[slot], pp_recv.at[p, h], other_core)

    def add_up(dst, terms, size):
        step = chunk_of(size, 2304)

        @pl.loop(0, size // step)
        def _(k):
            at = pl.multiple_of(k * step, LANES)
            total = terms[0](at, step).astype(jnp.float32)
            for term in terms[1:]:
                total += term(at, step).astype(jnp.float32)
            dst(at, step, total.astype(jnp.bfloat16))

    def run(op, z, slot_of):
        kind, t, h = op[:3]
        p = actual(t)
        towards = 1 if t > z else -1
        sides = [s for s in (1, -1) if 0 <= z + s < PLANES]
        if kind in ("zA", "zB", "yA", "yB", "pa", "yr"):
            send(op).start()
        elif kind == "wzA":
            send(("zA", t, h, 1)).wait_recv()
        elif kind == "wzB":
            send(("zB", t, h, 1)).wait_recv()
        elif kind == "wyA":
            send(("yA", t, h)).wait_recv()
        elif kind == "wyB":
            send(("yB", t, h)).wait_recv()
        elif kind == "S":
            slot = slot_of[(t, h)]
            pp(p, h, slot).wait_recv()

            def joined(at, step, value):
                pin[p, h, :, pl.ds(at, step)] = value

            add_up(
                joined,
                (
                    lambda at, step: own[slot, :, pl.ds(at, step)],
                    lambda at, step: pin[p, h, :, pl.ds(at, step)],
                ),
                width,
            )
        elif kind == "TB":
            if 0 <= z - towards < PLANES:
                up, place = sums(t, towards)
                send(("TB", t, h, towards)).wait_recv()

                def passed(at, step, value):
                    pin[p, h, :, pl.ds(wa + at, step)] = value

                add_up(
                    passed,
                    (
                        lambda at, step: pin[p, h, :, pl.ds(wa + at, step)],
                        lambda at, step: rs_b[up, place, h, :, pl.ds(at, step)],
                    ),
                    width - wa,
                )
            send(("TB", t, h, towards)).start()
        elif kind == "TA":
            up, place = sums(t, towards)
            send(("yr", t, h)).wait_recv()
            terms = [
                lambda at, step: pin[p, h, first, pl.ds(at, step)],
                lambda at, step: yr_a[p, h, :, pl.ds(at, step)],
            ]
            if 0 <= z - towards < PLANES:
                send(("TA", t, h, towards)).wait_recv()
                terms.append(lambda at, step: rs_a[up, place, h, :, pl.ds(at, step)])

            def passed(at, step, value):
                pin[p, h, first, pl.ds(at, step)] = value

            add_up(passed, terms, wa)
            send(("TA", t, h, towards)).start()
        elif kind == "FB1":
            terms = [lambda at, step: pin[p, h, second, pl.ds(wa + at, step)]]
            for s in sides:
                up, place = sums(t, -s)
                send(("TB", t, h, -s)).wait_recv()
                terms.append(
                    lambda at, step, up=up, place=place: rs_b[up, place, h, second, pl.ds(at, step)]
                )

            def passed(at, step, value):
                pin[p, h, second, pl.ds(wa + at, step)] = value

            add_up(passed, terms, width - wa)
            send(op).start()
        elif kind == "FB0":
            send(("FB1", t, h)).wait_recv()
            terms = [
                lambda at, step: pin[p, h, first, pl.ds(wa + at, step)],
                lambda at, step: yr_b[h, :, pl.ds(at, step)],
            ]
            for s in sides:
                up, place = sums(t, -s)
                terms.append(
                    lambda at, step, up=up, place=place: rs_b[up, place, h, first, pl.ds(at, step)]
                )

            def finished(at, step, value):
                out[pl.ds(h * rows, rows), pl.ds(wa + at, step)] = value

            add_up(finished, terms, width - wa)
        elif kind == "FA":
            send(("yr", t, h)).wait_recv()
            terms = [
                lambda at, step: pin[p, h, first, pl.ds(at, step)],
                lambda at, step: yr_a[p, h, :, pl.ds(at, step)],
            ]
            for s in sides:
                up, place = sums(t, -s)
                send(("TA", t, h, -s)).wait_recv()
                terms.append(
                    lambda at, step, up=up, place=place: rs_a[up, place, h, :, pl.ds(at, step)]
                )

            def finished(at, step, value):
                out[pl.ds(h * rows, rows), pl.ds(at, step)] = value

            add_up(finished, terms, wa)

    def compute(k, p, h):
        slot = k % 2
        for side in range(2):
            copy(
                x.at[p, h, pl.ds(side * rows, rows)], x.at[p, h, pl.ds((2 + side) * rows, rows)],
                pa_send.at[p, h, side], pa_recv.at[p, h, side], other_core,
            ).wait_recv()

        @pl.when(k == 0)
        def _():
            loads[0].wait()
            loads[1].wait()

        @pl.when(k >= 2)
        def _():
            pp(p, h, slot).wait_send()

        gate = jnp.dot(x[p, h, :, pl.ds(0, width)], wg[...], preferred_element_type=jnp.float32)
        up = jnp.dot(x[p, h, :, pl.ds(0, width)], wu[...], preferred_element_type=jnp.float32)
        hidden = (gate / (1.0 + jnp.exp(-gate)) * up).astype(jnp.bfloat16)
        table = x[p, h, :, pl.ds(width, LANES)].astype(jnp.float32)
        lane = lax.broadcasted_iota(jnp.int32, table.shape, 1)
        scale = jnp.sum(jnp.where(lane == node, table, 0.0), axis=1, keepdims=True)

        @pl.when(k == 0)
        def _():
            loads[2].wait()

        step = chunk_of(width, 1792)
        for c in range(width // step):
            cols = pl.ds(c * step, step)
            value = jnp.dot(hidden, wd[:, cols], preferred_element_type=jnp.float32) * scale
            own[slot, :, cols] = value[:2 * rows]
            pout[slot, :, cols] = value[2 * rows:].astype(jnp.bfloat16)
        pp(p, h, slot).start()

    items = [[group[-1][1:3] for group in groups[:-1]] for groups in SCHEDULE]
    count = len(items[0])

    @pl.loop(0, count)
    def _(k):
        for z, groups in enumerate(SCHEDULE):
            slot_of = {item: i % 2 for i, item in enumerate(items[z])}
            for i, group in enumerate(groups[:-1]):

                @pl.when((near == z) & (k == i))
                def _(group=group, z=z, slot_of=slot_of):
                    for op in group[:-1]:
                        run(op, z, slot_of)

        t, h = 0, 0
        for z, of in enumerate(items):
            for i, item in enumerate(of):
                here = jnp.where(near == z, 1, 0) * jnp.where(k == i, 1, 0)
                t, h = t + here * item[0], h + here * item[1]
        compute(k, actual(t), h)

    for z, groups in enumerate(SCHEDULE):
        slot_of = {item: i % 2 for i, item in enumerate(items[z])}

        @pl.when(near == z)
        def _(groups=groups, z=z, slot_of=slot_of):
            for op in groups[-1]:
                run(op, z, slot_of)
            for group in groups:
                for op in group:
                    if op[0] in ("zA", "zB", "yA", "yB", "pa", "yr", "FB1"):
                        send(op).wait_send()
                    elif op[0] in ("TA", "TB"):
                        send((*op, 1 if op[1] > z else -1)).wait_send()
            for t, h in items[z][-2:]:
                pp(actual(t), h, slot_of[(t, h)]).wait_send()


def buffers(tok, width, hid):
    wa = single_columns(width)
    rows = tok // SLICES
    kind = jnp.bfloat16
    return [
        pltpu.VMEM((PLANES, SLICES, 4 * rows, width + LANES), kind),
        pltpu.VMEM((width, hid), kind),
        pltpu.VMEM((width, hid), kind),
        pltpu.VMEM((hid, width), kind),
        pltpu.VMEM((PLANES, SLICES, 2 * rows, width), kind),
        pltpu.VMEM((2, 2 * rows, width), kind),
        pltpu.VMEM((2, 2 * rows, width), jnp.float32),
        pltpu.VMEM((2, PLANES - 1, SLICES, rows, wa), kind),
        pltpu.VMEM((2, PLANES - 1, SLICES, 2 * rows, width - wa), kind),
        pltpu.VMEM((PLANES, SLICES, rows, wa), kind),
        pltpu.VMEM((SLICES, rows, width - wa), kind),
    ]


def by_trees(tokens, gate_ids, gate_values, w_gate, w_up, w_down):
    tok, width = tokens.shape
    anywhere = pl.BlockSpec(memory_space=pl.ANY)
    in_vmem = pl.BlockSpec(memory_space=pltpu.VMEM)

    def dma(*shape):
        return pltpu.SemaphoreType.DMA(shape)

    each = (PLANES, SLICES)
    return pl.pallas_call(
        tree_kernel,
        out_shape=jax.ShapeDtypeStruct((tok, width), jnp.bfloat16),
        in_specs=[anywhere, in_vmem, in_vmem, anywhere, anywhere, anywhere],
        out_specs=in_vmem,
        scratch_shapes=[
            *buffers(tok, width, w_gate.shape[2]),
            dma(3), dma(SLICES), dma(2, *each), dma(*each), dma(2, *each), dma(*each),
            dma(*each), dma(*each), dma(SLICES), dma(SLICES),
            dma(*each, 2), dma(*each, 2), dma(2), dma(*each),
            dma(*each), dma(2, *each), dma(*each), dma(2, *each),
            dma(*each), dma(*each), dma(SLICES), dma(SLICES),
        ],
        compiler_params=pltpu.CompilerParams(
            collective_id=0, has_side_effects=True, vmem_limit_bytes=VMEM_LIMIT
        ),
    )(tokens, gate_ids.T, gate_values.T, w_gate[0], w_up[0], w_down[0])


def by_collectives(tokens, gate_ids, gate_values, w_gate, w_up, w_down):
    n = lax.axis_size("node")
    every = ("node", "local")
    weights = lax.all_gather(expert_weights(gate_ids, gate_values, n), every, axis=0, tiled=True)
    rows = lax.all_gather(tokens, every, axis=0, tiled=True)
    mine = (jnp.arange(n, dtype=jnp.int32) == lax.axis_index("node"))[None, :]
    scale = jnp.sum(jnp.where(mine, weights.astype(jnp.float32), 0.0), axis=1, keepdims=True)
    gate_act = jnp.dot(rows, w_gate[0], preferred_element_type=jnp.float32)
    up_act = jnp.dot(rows, w_up[0], preferred_element_type=jnp.float32)
    hidden = (jax.nn.silu(gate_act) * up_act).astype(jnp.bfloat16)
    partial_value = jnp.dot(hidden, w_down[0], preferred_element_type=jnp.float32) * scale
    return lax.psum_scatter(
        partial_value.astype(jnp.bfloat16), every, scatter_dimension=0, tiled=True
    )


def trees_fit(n, tok, width, hid):
    if n != PLANES * COLUMNS or lax.axis_size("local") != 2 or tok % (16 * SLICES) or width % LANES:
        return False
    if width < 2 * LANES:
        return False
    size = 2 * tok * width + 2**21
    for ref in buffers(tok, width, hid):
        size += ref.inner_aval.size * ref.inner_aval.dtype.itemsize
    return size < VMEM_LIMIT


def per_device(tokens, gate_ids, gate_values, w_gate, w_up, w_down):
    n = lax.axis_size("node")
    args = (tokens, gate_ids, gate_values, w_gate, w_up, w_down)
    if trees_fit(n, tokens.shape[0], tokens.shape[1], w_gate.shape[2]):
        return by_trees(*args)
    return by_collectives(*args)


def solution(mesh):
    return jax.shard_map(
        per_device,
        mesh=mesh,
        in_specs=(
            P(("rep", "node", "local"), None),
            P(("rep", "node", "local"), None),
            P(("rep", "node", "local"), None),
            P("node", None, "local"),
            P("node", None, "local"),
            P("node", "local", None),
        ),
        out_specs=P(("rep", "node", "local"), None),
        check_vma=False,
    )
```

```python
import functools

import jax
import jax.numpy as jnp
from jax import lax
from jax.experimental import pallas as pl
from jax.experimental.pallas import tpu as pltpu
from jax.sharding import PartitionSpec as P

MESH = pl.DeviceIdType.MESH
LANES = 128
VMEM_LIMIT = 67_000_000
PLANES = 4
COLUMNS = 2
SLICES = 2
SINGLE = (34, 56)
PIECES = 2

SCHEDULE = (
    (
        (("yB", 0, 1), ("yA", 0, 0, 0), ("yB", 0, 0), ("zA", 0, 1, 1, 1), ("zA", 0, 0, 1, 1), ("zA", 0, 0, 0, 1), ("wyB", 0, 1), ("wzA", 1, 1, 0), ("zA", 0, 1, 0, 1), ("yA", 1, 1, 0), ("wyB", 0, 0), ("zB", 0, 0, 0, 1), ("wzB", 1, 1, 0), ("wzA", 1, 1, 1), ("yA", 1, 1, 1), ("zB", 0, 0, 1, 1), ("yA", 0, 0, 1), ("wyA", 1, 1, 1), ("zB", 0, 1, 0, 1), ("wzA", 2, 1, 0), ("wzB", 1, 1, 1), ("yA", 2, 1, 0), ("wyA", 1, 1, 0), ("pa", 1, 1, 1), ("pa", 1, 1, 0), ("wzA", 2, 1, 1), ("zB", 0, 1, 1, 1), ("yA", 2, 1, 1), ("yA", 0, 1, 1), ("C", 1, 1),),
        (("yA", 0, 1, 0), ("wyA", 2, 1, 0), ("wyA", 0, 0, 0), ("S", 1, 1), ("TB", 1, 1, 0), ("wzB", 2, 1, 0), ("wzB", 2, 1, 1), ("pa", 2, 1, 0), ("wyA", 2, 1, 1), ("pa", 2, 1, 1), ("yr", 1, 1, 1), ("yr", 1, 1, 0), ("wzA", 3, 0, 1), ("wyA", 0, 1, 1), ("pa", 0, 0, 0), ("pa", 0, 1, 0), ("wyA", 0, 0, 1), ("TB", 1, 1, 1), ("C", 2, 1),),
        (("TA", 1, 1, 1), ("wzA", 3, 0, 0), ("yA", 3, 0, 1), ("pa", 0, 0, 1), ("yA", 3, 0, 0), ("S", 2, 1), ("TB", 2, 1, 0), ("wzB", 3, 0, 0), ("yr", 2, 1, 1), ("pa", 3, 0, 0), ("C", 0, 0),),
        (("TA", 1, 1, 0), ("wyA", 3, 0, 1), ("wyA", 3, 0, 0), ("TB", 2, 1, 1), ("wzB", 3, 0, 1), ("yr", 2, 1, 0), ("pa", 3, 0, 1), ("wzA", 3, 1, 0), ("wyA", 0, 1, 0), ("yA", 3, 1, 0), ("TA", 2, 1, 1), ("C", 3, 0),),
        (("wzA", 3, 1, 1), ("yA", 3, 1, 1), ("TA", 2, 1, 0), ("S", 3, 0), ("yr", 3, 0, 1), ("wzA", 2, 0, 1), ("S", 0, 0), ("wyA", 3, 1, 0), ("TB", 3, 0, 1), ("pa", 0, 1, 1), ("wyA", 3, 1, 1), ("wzB", 3, 1, 0), ("yA", 2, 0, 1), ("wzB", 3, 1, 1), ("pa", 3, 1, 1), ("pa", 3, 1, 0), ("TB", 3, 0, 0), ("TA", 3, 0, 1), ("yr", 3, 0, 0), ("wzA", 2, 0, 0), ("yA", 2, 0, 0), ("C", 3, 1),),
        (("TA", 3, 0, 0), ("wyA", 2, 0, 1), ("wzB", 2, 0, 1), ("yr", 0, 0, 1), ("S", 3, 1), ("TB", 3, 1, 0), ("wyA", 2, 0, 0), ("yr", 3, 1, 1), ("pa", 2, 0, 1), ("C", 0, 1),),
        (("yr", 3, 1, 0), ("wzA", 1, 0, 1), ("TB", 3, 1, 1), ("wzB", 2, 0, 0), ("pa", 2, 0, 0), ("TA", 3, 1, 1), ("yA", 1, 0, 1), ("wzA", 1, 0, 0), ("yA", 1, 0, 0), ("C", 2, 0),),
        (("TA", 3, 1, 0), ("S", 0, 1), ("wzB", 1, 0, 0), ("wyA", 1, 0, 1), ("yr", 0, 0, 0), ("S", 2, 0), ("TB", 2, 0, 0), ("yr", 2, 0, 0), ("wzB", 1, 0, 1), ("pa", 1, 0, 0), ("wyA", 1, 0, 0), ("yr", 2, 0, 1), ("pa", 1, 0, 1), ("TB", 2, 0, 1), ("yr", 0, 1, 0), ("C", 1, 0),),
        (("TA", 2, 0, 0), ("FB1", 0, 0), ("TA", 2, 0, 1), ("S", 1, 0), ("yr", 1, 0, 0), ("TB", 1, 0, 1), ("yr", 1, 0, 1), ("TB", 1, 0, 0), ("TA", 1, 0, 0), ("FB1", 0, 1), ("FB0", 0, 0), ("yr", 0, 1, 1), ("TA", 1, 0, 1), ("FA", 0, 0, 1), ("FA", 0, 1, 0), ("FA", 0, 0, 0), ("FB0", 0, 1), ("FA", 0, 1, 1),),
    ),
    (
        (("zA", 1, 1, 1, -1), ("zA", 1, 1, 0, -1), ("zB", 1, 1, 0, -1), ("zA", 1, 1, 0, 1), ("yB", 1, 1), ("zA", 1, 1, 1, 1), ("yA", 1, 1, 0), ("wzA", 2, 1, 0), ("wyB", 1, 1), ("yB", 1, 0), ("zB", 1, 1, 1, 1), ("zB", 1, 1, 1, -1), ("zB", 1, 1, 0, 1), ("yA", 1, 1, 1), ("wzA", 2, 1, 1), ("yA", 2, 1, 0), ("wyB", 1, 0), ("wzA", 0, 0, 1), ("wzB", 2, 1, 1), ("zA", 1, 0, 1, 1), ("zA", 2, 1, 0, -1), ("zA", 0, 0, 1, 1), ("wzA", 0, 1, 1), ("wzA", 0, 1, 0), ("yA", 2, 1, 1), ("zA", 2, 1, 1, -1), ("wzB", 0, 0, 0), ("zB", 2, 1, 1, -1), ("wzA", 0, 0, 0), ("yA", 0, 0, 1), ("wzB", 2, 1, 0), ("wyA", 2, 1, 0), ("zA", 0, 0, 0, 1), ("yA", 1, 0, 0), ("zB", 0, 0, 0, 1), ("wzA", 3, 0, 1), ("pa", 1, 1, 0), ("wyA", 2, 1, 1), ("wyA", 1, 1, 0), ("zB", 2, 1, 0, -1), ("zA", 3, 0, 1, -1), ("yA", 0, 0, 0), ("wzA", 3, 0, 0), ("wzB", 0, 0, 1), ("zA", 0, 1, 0, 1), ("zB", 0, 0, 1, 1), ("zA", 3, 0, 0, -1), ("wyA", 1, 1, 1), ("zA", 0, 1, 1, 1), ("wzB", 3, 0, 0), ("pa", 1, 1, 1), ("yA", 3, 0, 1), ("yA", 0, 1, 1), ("yA", 0, 1, 0), ("zB", 3, 0, 0, -1), ("zA", 1, 0, 0, 1), ("pa", 2, 1, 0), ("C", 1, 1),),
        (("wzB", 0, 1, 0), ("wzA", 3, 1, 0), ("zA", 3, 1, 0, -1), ("yA", 3, 0, 0), ("pa", 0, 1, 0), ("yA", 3, 1, 0), ("wzB", 0, 1, 1), ("wyA", 0, 1, 1), ("wzB", 3, 0, 1), ("wzA", 2, 0, 1), ("pa", 2, 1, 1), ("zB", 0, 1, 0, 1), ("zB", 3, 0, 1, -1), ("zA", 2, 0, 1, -1), ("yA", 1, 0, 1), ("C", 2, 1),),
        (("pa", 0, 0, 0), ("wyA", 0, 1, 0), ("zB", 0, 1, 1, 1), ("pa", 0, 1, 1), ("wzA", 3, 1, 1), ("zB", 1, 0, 1, 1), ("wyA", 1, 0, 0), ("zA", 3, 1, 1, -1), ("wzB", 3, 1, 0), ("wyA", 3, 0, 0), ("wzA", 2, 0, 0), ("yA", 2, 0, 1), ("pa", 3, 0, 0), ("S", 1, 1), ("S", 2, 1), ("zB", 1, 0, 0, 1), ("yr", 2, 1, 1), ("zB", 3, 1, 0, -1), ("wyA", 3, 0, 1), ("wyA", 1, 0, 1), ("TB", 2, 1, 0), ("pa", 1, 0, 1), ("wzB", 3, 1, 1), ("pa", 3, 0, 1), ("wyA", 0, 0, 1), ("yA", 3, 1, 1), ("zB", 3, 1, 1, -1), ("C", 0, 1),),
        (("wyA", 0, 0, 0), ("yA", 2, 0, 0), ("yr", 2, 1, 0), ("pa", 3, 1, 0), ("TB", 2, 1, 1), ("zA", 2, 0, 0, -1), ("C", 3, 0),),
        (("wzB", 2, 0, 1), ("wyA", 3, 1, 1), ("TA", 2, 1, 1), ("wzB", 2, 0, 0), ("zB", 2, 0, 1, -1), ("S", 3, 0), ("pa", 2, 0, 0), ("yr", 3, 0, 0), ("TB", 3, 0, 1), ("zA", 1, 0, 1, -1), ("pa", 0, 0, 1), ("yr", 3, 0, 1), ("S", 0, 1), ("zB", 2, 0, 0, -1), ("wyA", 3, 1, 0), ("yr", 1, 1, 1), ("zA", 1, 0, 0, -1), ("pa", 1, 0, 0), ("wyA", 2, 0, 1), ("wyA", 2, 0, 0), ("zB", 1, 0, 0, -1), ("pa", 3, 1, 1), ("pa", 2, 0, 1), ("TB", 3, 0, 0), ("yr", 1, 1, 0), ("TA", 2, 1, 0), ("C", 3, 1),),
        (("yr", 0, 1, 1), ("yr", 0, 1, 0), ("C", 0, 0),),
        (("TA", 3, 0, 1), ("TA", 3, 0, 0), ("zB", 1, 0, 1, -1), ("S", 3, 1), ("yr", 3, 1, 0), ("S", 0, 0), ("yr", 0, 0, 0), ("TB", 0, 0, 0), ("TB", 3, 1, 0), ("C", 2, 0),),
        (("TB", 3, 1, 1), ("yr", 0, 0, 1), ("yr", 3, 1, 1), ("FA", 1, 1, 0), ("TA", 3, 1, 0), ("TB", 0, 0, 1), ("FB1", 1, 1), ("TB", 0, 1, 0), ("C", 1, 0),),
        (("S", 2, 0), ("TB", 0, 1, 1), ("TB", 2, 0, 1), ("TB", 2, 0, 0), ("yr", 2, 0, 1), ("yr", 2, 0, 0), ("TA", 3, 1, 1), ("S", 1, 0), ("TA", 0, 0, 1), ("TA", 0, 1, 0), ("yr", 1, 0, 0), ("TA", 2, 0, 0), ("FB1", 1, 0), ("yr", 1, 0, 1), ("TA", 2, 0, 1), ("TA", 0, 0, 0), ("TA", 0, 1, 1), ("FB0", 1, 1), ("FA", 1, 0, 0), ("FA", 1, 1, 1), ("FB0", 1, 0), ("FA", 1, 0, 1),),
    ),
)


def chunk_of(size, most=1024):
    chunk = most
    while size % chunk:
        chunk -= LANES
    return chunk


def expert_weights(gate_ids, gate_values, columns):
    expert_row = jnp.arange(columns, dtype=jnp.int32)
    return jnp.sum(
        jnp.where(
            gate_ids[:, :, None] == expert_row[None, None, :],
            gate_values.astype(jnp.float32)[:, :, None],
            jnp.float32(0.0),
        ),
        axis=1,
    ).astype(jnp.bfloat16)


def single_columns(width):
    return max(LANES, width * SINGLE[0] // (SINGLE[1] * LANES) * LANES)


def tree_kernel(
    tokens, ids, values, wg_hbm, wu_hbm, wd_hbm, out,
    x, wg, wu, wd, pin, pout, own, rs_a, rs_b, yr_a, yr_b,
    weight_sem, own_sem, za_send, za_recv, zb_send, zb_recv, ya_send, ya_recv, yb_send, yb_recv,
    pa_send, pa_recv, pp_send, pp_recv, ra_send, ra_recv, rb_send, rb_recv,
    yra_send, yra_recv, yrb_send, yrb_recv,
):
    tok, width = tokens.shape
    wa = single_columns(width)
    rows = tok // SLICES
    node = lax.axis_index("node")
    other_core = {"local": 1 - lax.axis_index("local")}
    plane, column = node // COLUMNS, node % COLUMNS
    across = {"node": node + 1 - 2 * column}
    flip = jnp.where(plane >= PLANES // 2, 1, 0)
    near = plane * (1 - flip) + (PLANES - 1 - plane) * flip

    def actual(t):
        return t * (1 - flip) + (PLANES - 1 - t) * flip

    def along(s):
        return {"node": node + COLUMNS * s * (1 - 2 * flip)}

    def upward(s):
        return (1 - flip) if s > 0 else flip

    cols_b, cols_bt = pl.ds(wa, width - wa), pl.ds(wa, width + LANES - wa)
    bounds = [wa // LANES * j // PIECES * LANES for j in range(PIECES + 1)]
    cols_a = [pl.ds(bounds[j], bounds[j + 1] - bounds[j]) for j in range(PIECES)]

    keeps = [
        pltpu.make_async_copy(
            tokens.at[pl.ds(h * rows, rows)],
            x.at[plane, h, pl.ds(0, rows), pl.ds(0, width)],
            own_sem.at[h],
        )
        for h in range(SLICES)
    ]
    for keep in keeps:
        keep.start()
    loads = [
        pltpu.make_async_copy(src, dst, weight_sem.at[k])
        for k, (src, dst) in enumerate(((wg_hbm, wg), (wu_hbm, wu), (wd_hbm, wd)))
    ]

    barrier = pltpu.get_barrier_semaphore()
    for target in (other_core, across, along(1)):
        pl.semaphore_signal(barrier, inc=1, device_id=target, device_id_type=MESH)

    @pl.when(near > 0)
    def _():
        pl.semaphore_signal(barrier, inc=1, device_id=along(-1), device_id_type=MESH)

    table_row = lax.broadcasted_iota(jnp.int32, (LANES, tok), 0)
    turned = jnp.zeros((LANES, tok), jnp.float32)
    for choice in range(ids.shape[0]):
        chosen = table_row == ids[pl.ds(choice, 1), :]
        turned += jnp.where(chosen, values[pl.ds(choice, 1), :].astype(jnp.float32), 0.0)
    ones = lax.broadcasted_iota(jnp.int32, (tok, tok), 0) == lax.broadcasted_iota(
        jnp.int32, (tok, tok), 1
    )
    table = lax.dot_general(
        jnp.where(ones, 1.0, 0.0).astype(jnp.bfloat16), turned.astype(jnp.bfloat16),
        (((1,), (1,)), ((), ())), preferred_element_type=jnp.float32,
    ).astype(jnp.bfloat16)
    for h in range(SLICES):
        x[plane, h, pl.ds(0, rows), pl.ds(width, LANES)] = table[h * rows:(h + 1) * rows]
    for keep in keeps:
        keep.wait()
    for load in loads:
        load.start()
    pl.semaphore_wait(barrier, 3 + jnp.where(near > 0, 1, 0))

    first, second = pl.ds(0, rows), pl.ds(rows, rows)
    part = (first, second)

    def copy(src, dst, send, recv, target):
        return pltpu.make_async_remote_copy(
            src_ref=src, dst_ref=dst, send_sem=send, recv_sem=recv,
            device_id=target, device_id_type=MESH,
        )

    def sums(t, s):
        up = upward(s)
        return up, actual(t) - up

    def send(op):
        kind, t, h = op[:3]
        p = actual(t)
        if kind == "zA":
            j, s = op[3:]
            ref = x.at[p, h, first, cols_a[j]]
            return copy(ref, ref, za_send.at[max(s, 0), p, h, j], za_recv.at[p, h, j], along(s))
        if kind == "zB":
            j, s = op[3:]
            ref = x.at[p, h, part[j], cols_bt]
            return copy(ref, ref, zb_send.at[max(s, 0), p, h, j], zb_recv.at[p, h, j], along(s))
        if kind == "yA":
            j = op[3]
            return copy(
                x.at[p, h, first, cols_a[j]], x.at[p, h, second, cols_a[j]],
                ya_send.at[p, h, j], ya_recv.at[p, h, j], across,
            )
        if kind == "yB":
            return copy(
                x.at[p, h, first, cols_bt], x.at[p, h, second, cols_bt],
                yb_send.at[h], yb_recv.at[h], across,
            )
        if kind == "pa":
            return copy(
                x.at[p, h, part[op[3]]], x.at[p, h, pl.ds((2 + op[3]) * rows, rows)],
                pa_send.at[p, h, op[3]], pa_recv.at[p, h, op[3]], other_core,
            )
        if kind == "yr":
            j = op[3]
            return copy(
                pin.at[p, h, second, cols_a[j]], yr_a.at[p, h, :, cols_a[j]],
                yra_send.at[p, h, j], yra_recv.at[p, h, j], across,
            )
        if kind == "FB1":
            return copy(
                pin.at[p, h, second, cols_b], yr_b.at[h], yrb_send.at[h], yrb_recv.at[h], across
            )
        j, s = op[3:]
        up, place = sums(t, s)
        if kind == "TA":
            return copy(
                pin.at[p, h, first, cols_a[j]], rs_a.at[up, place, h, :, cols_a[j]],
                ra_send.at[p, h, j], ra_recv.at[up, p, h, j], along(s),
            )
        return copy(
            pin.at[p, h, part[j], cols_b], rs_b.at[up, place, h, part[j]],
            rb_send.at[p, h, j], rb_recv.at[up, p, h, j], along(s),
        )

    def pp(p, h, slot):
        return copy(pout.at[slot], pin.at[p, h], pp_send.at[slot], pp_recv.at[p, h], other_core)

    def add_up(dst, terms, size):
        step = chunk_of(size, 2304)

        @pl.loop(0, size // step)
        def _(k):
            at = pl.multiple_of(k * step, LANES)
            total = terms[0](at, step).astype(jnp.float32)
            for term in terms[1:]:
                total += term(at, step).astype(jnp.float32)
            dst(at, step, total.astype(jnp.bfloat16))

    def run(op, z, slot_of):
        kind, t, h = op[:3]
        p = actual(t)
        towards = 1 if t > z else -1
        sides = [s for s in (1, -1) if 0 <= z + s < PLANES]
        if kind in ("zA", "zB", "yA", "yB", "pa", "yr"):
            send(op).start()
        elif kind == "wzA":
            send(("zA", t, h, op[3], 1)).wait_recv()
        elif kind == "wzB":
            send(("zB", t, h, op[3], 1)).wait_recv()
        elif kind == "wyA":
            send(("yA", *op[1:])).wait_recv()
        elif kind == "wyB":
            send(("yB", t, h)).wait_recv()
        elif kind == "S":
            slot = slot_of[(t, h)]
            pp(p, h, slot).wait_recv()

            def joined(at, step, value):
                pin[p, h, :, pl.ds(at, step)] = value

            add_up(
                joined,
                (
                    lambda at, step: own[slot, :, pl.ds(at, step)],
                    lambda at, step: pin[p, h, :, pl.ds(at, step)],
                ),
                width,
            )
        elif kind == "TB":
            j = op[3]
            if 0 <= z - towards < PLANES:
                up, place = sums(t, towards)
                send((*op, towards)).wait_recv()

                def passed(at, step, value):
                    pin[p, h, part[j], pl.ds(wa + at, step)] = value

                add_up(
                    passed,
                    (
                        lambda at, step: pin[p, h, part[j], pl.ds(wa + at, step)],
                        lambda at, step: rs_b[up, place, h, part[j], pl.ds(at, step)],
                    ),
                    width - wa,
                )
            send((*op, towards)).start()
        elif kind in ("TA", "FA"):
            j = op[3]
            send(("yr", *op[1:])).wait_recv()
            terms = [
                lambda at, step: pin[p, h, first, pl.ds(bounds[j] + at, step)],
                lambda at, step: yr_a[p, h, :, pl.ds(bounds[j] + at, step)],
            ]
            own_plane = kind == "FA"
            for s in [-s for s in sides] if own_plane else [towards]:
                if own_plane or 0 <= z - towards < PLANES:
                    up, place = sums(t, s)
                    send(("TA", t, h, j, s)).wait_recv()
                    terms.append(
                        lambda at, step, up=up, place=place: rs_a[
                            up, place, h, :, pl.ds(bounds[j] + at, step)
                        ]
                    )

            def finished(at, step, value):
                if own_plane:
                    out[pl.ds(h * rows, rows), pl.ds(bounds[j] + at, step)] = value
                else:
                    pin[p, h, first, pl.ds(bounds[j] + at, step)] = value

            add_up(finished, terms, bounds[j + 1] - bounds[j])
            if not own_plane:
                send((*op, towards)).start()
        elif kind in ("FB0", "FB1"):
            j = int(kind == "FB1")
            terms = [lambda at, step: pin[p, h, part[j], pl.ds(wa + at, step)]]
            if j == 0:
                send(("FB1", t, h)).wait_recv()
                terms.append(lambda at, step: yr_b[h, :, pl.ds(at, step)])
            for s in sides:
                up, place = sums(t, -s)
                send(("TB", t, h, j, -s)).wait_recv()
                terms.append(
                    lambda at, step, up=up, place=place: rs_b[
                        up, place, h, part[j], pl.ds(at, step)
                    ]
                )

            def settled(at, step, value):
                if j == 0:
                    out[pl.ds(h * rows, rows), pl.ds(wa + at, step)] = value
                else:
                    pin[p, h, second, pl.ds(wa + at, step)] = value

            add_up(settled, terms, width - wa)
            if j == 1:
                send(op).start()

    def compute(k, p, h):
        slot = k % 2
        for side in range(2):
            copy(
                x.at[p, h, pl.ds(side * rows, rows)], x.at[p, h, pl.ds((2 + side) * rows, rows)],
                pa_send.at[p, h, side], pa_recv.at[p, h, side], other_core,
            ).wait_recv()

        @pl.when(k == 0)
        def _():
            loads[0].wait()
            loads[1].wait()

        @pl.when(k >= 2)
        def _():
            pp(p, h, slot).wait_send()

        gate = jnp.dot(x[p, h, :, pl.ds(0, width)], wg[...], preferred_element_type=jnp.float32)
        up = jnp.dot(x[p, h, :, pl.ds(0, width)], wu[...], preferred_element_type=jnp.float32)
        hidden = (gate / (1.0 + jnp.exp(-gate)) * up).astype(jnp.bfloat16)
        table = x[p, h, :, pl.ds(width, LANES)].astype(jnp.float32)
        lane = lax.broadcasted_iota(jnp.int32, table.shape, 1)
        scale = jnp.sum(jnp.where(lane == node, table, 0.0), axis=1, keepdims=True)

        @pl.when(k == 0)
        def _():
            loads[2].wait()

        step = chunk_of(width, 1792)
        for c in range(width // step):
            cols = pl.ds(c * step, step)
            value = jnp.dot(hidden, wd[:, cols], preferred_element_type=jnp.float32) * scale
            own[slot, :, cols] = value[:2 * rows]
            pout[slot, :, cols] = value[2 * rows:].astype(jnp.bfloat16)
        pp(p, h, slot).start()

    items = [[group[-1][1:3] for group in groups[:-1]] for groups in SCHEDULE]
    count = len(items[0])

    @pl.loop(0, count)
    def _(k):
        for z, groups in enumerate(SCHEDULE):
            slot_of = {item: i % 2 for i, item in enumerate(items[z])}
            for i, group in enumerate(groups[:-1]):

                @pl.when((near == z) & (k == i))
                def _(group=group, z=z, slot_of=slot_of):
                    for op in group[:-1]:
                        run(op, z, slot_of)

        t, h = 0, 0
        for z, of in enumerate(items):
            for i, item in enumerate(of):
                here = jnp.where(near == z, 1, 0) * jnp.where(k == i, 1, 0)
                t, h = t + here * item[0], h + here * item[1]
        compute(k, actual(t), h)

    for z, groups in enumerate(SCHEDULE):
        slot_of = {item: i % 2 for i, item in enumerate(items[z])}

        @pl.when(near == z)
        def _(groups=groups, z=z, slot_of=slot_of):
            for op in groups[-1]:
                run(op, z, slot_of)
            for group in groups:
                for op in group:
                    if op[0] in ("zA", "zB", "yA", "yB", "pa", "yr", "FB1"):
                        send(op).wait_send()
                    elif op[0] in ("TA", "TB"):
                        send((*op, 1 if op[1] > z else -1)).wait_send()
            for t, h in items[z][-2:]:
                pp(actual(t), h, slot_of[(t, h)]).wait_send()


def buffers(tok, width, hid):
    wa = single_columns(width)
    rows = tok // SLICES
    kind = jnp.bfloat16
    return [
        pltpu.VMEM((PLANES, SLICES, 4 * rows, width + LANES), kind),
        pltpu.VMEM((width, hid), kind),
        pltpu.VMEM((width, hid), kind),
        pltpu.VMEM((hid, width), kind),
        pltpu.VMEM((PLANES, SLICES, 2 * rows, width), kind),
        pltpu.VMEM((2, 2 * rows, width), kind),
        pltpu.VMEM((2, 2 * rows, width), jnp.float32),
        pltpu.VMEM((2, PLANES - 1, SLICES, rows, wa), kind),
        pltpu.VMEM((2, PLANES - 1, SLICES, 2 * rows, width - wa), kind),
        pltpu.VMEM((PLANES, SLICES, rows, wa), kind),
        pltpu.VMEM((SLICES, rows, width - wa), kind),
    ]


def by_trees(tokens, gate_ids, gate_values, w_gate, w_up, w_down):
    tok, width = tokens.shape
    anywhere = pl.BlockSpec(memory_space=pl.ANY)
    in_vmem = pl.BlockSpec(memory_space=pltpu.VMEM)

    def dma(*shape):
        return pltpu.SemaphoreType.DMA(shape)

    each = (PLANES, SLICES)
    return pl.pallas_call(
        tree_kernel,
        out_shape=jax.ShapeDtypeStruct((tok, width), jnp.bfloat16),
        in_specs=[anywhere, in_vmem, in_vmem, anywhere, anywhere, anywhere],
        out_specs=in_vmem,
        scratch_shapes=[
            *buffers(tok, width, w_gate.shape[2]),
            dma(3), dma(SLICES),
            dma(2, *each, PIECES), dma(*each, PIECES), dma(2, *each, 2), dma(*each, 2),
            dma(*each, PIECES), dma(*each, PIECES), dma(SLICES), dma(SLICES),
            dma(*each, 2), dma(*each, 2), dma(2), dma(*each),
            dma(*each, PIECES), dma(2, *each, PIECES), dma(*each, 2), dma(2, *each, 2),
            dma(*each, PIECES), dma(*each, PIECES), dma(SLICES), dma(SLICES),
        ],
        compiler_params=pltpu.CompilerParams(
            collective_id=0, has_side_effects=True, vmem_limit_bytes=VMEM_LIMIT
        ),
    )(tokens, gate_ids.T, gate_values.T, w_gate[0], w_up[0], w_down[0])


def by_collectives(tokens, gate_ids, gate_values, w_gate, w_up, w_down):
    n = lax.axis_size("node")
    every = ("node", "local")
    weights = lax.all_gather(expert_weights(gate_ids, gate_values, n), every, axis=0, tiled=True)
    rows = lax.all_gather(tokens, every, axis=0, tiled=True)
    mine = (jnp.arange(n, dtype=jnp.int32) == lax.axis_index("node"))[None, :]
    scale = jnp.sum(jnp.where(mine, weights.astype(jnp.float32), 0.0), axis=1, keepdims=True)
    gate_act = jnp.dot(rows, w_gate[0], preferred_element_type=jnp.float32)
    up_act = jnp.dot(rows, w_up[0], preferred_element_type=jnp.float32)
    hidden = (jax.nn.silu(gate_act) * up_act).astype(jnp.bfloat16)
    partial_value = jnp.dot(hidden, w_down[0], preferred_element_type=jnp.float32) * scale
    return lax.psum_scatter(
        partial_value.astype(jnp.bfloat16), every, scatter_dimension=0, tiled=True
    )


def trees_fit(n, tok, width, hid):
    if n != PLANES * COLUMNS or lax.axis_size("local") != 2 or tok % (16 * SLICES) or width % LANES:
        return False
    if width < 2 * LANES:
        return False
    size = 2 * tok * width + 2**21
    for ref in buffers(tok, width, hid):
        size += ref.inner_aval.size * ref.inner_aval.dtype.itemsize
    return size < VMEM_LIMIT


def per_device(tokens, gate_ids, gate_values, w_gate, w_up, w_down):
    n = lax.axis_size("node")
    args = (tokens, gate_ids, gate_values, w_gate, w_up, w_down)
    if trees_fit(n, tokens.shape[0], tokens.shape[1], w_gate.shape[2]):
        return by_trees(*args)
    return by_collectives(*args)


def solution(mesh):
    return jax.shard_map(
        per_device,
        mesh=mesh,
        in_specs=(
            P(("rep", "node", "local"), None),
            P(("rep", "node", "local"), None),
            P(("rep", "node", "local"), None),
            P("node", None, "local"),
            P("node", None, "local"),
            P("node", "local", None),
        ),
        out_specs=P(("rep", "node", "local"), None),
        check_vma=False,
    )
```

```python
import functools

import jax
import jax.numpy as jnp
from jax import lax
from jax.experimental import pallas as pl
from jax.experimental.pallas import tpu as pltpu
from jax.sharding import PartitionSpec as P

MESH = pl.DeviceIdType.MESH
LANES = 128
VMEM_LIMIT = 67_000_000
PLANES = 4
COLUMNS = 2
SLICES = 2
SINGLE = (34, 56)
PIECES = 3

SCHEDULE = (
    (
        (("yA", 0, 1, 1), ("zA", 0, 0, 1, 1), ("yT", 0, 0), ("zA", 0, 1, 0, 1), ("yB", 0, 1), ("zA", 0, 1, 2, 1), ("wyT", 0, 0), ("zA", 0, 1, 1, 1), ("wzA", 1, 0, 1), ("yA", 1, 0, 1), ("yB", 0, 0), ("zA", 0, 0, 2, 1), ("zT", 0, 0, 1), ("wyB", 0, 1), ("wzA", 1, 0, 0), ("zB", 0, 1, 1, 1), ("zB", 0, 0, 0, 1), ("yA", 1, 0, 0), ("wzA", 1, 0, 2), ("yA", 0, 1, 0), ("yA", 1, 0, 2), ("yA", 0, 1, 2), ("wzB", 1, 0, 0), ("yA", 0, 0, 0), ("wyA", 1, 0, 0), ("wzT", 1, 0), ("zA", 0, 0, 0, 1), ("paT", 0, 0), ("paT", 1, 0), ("wyB", 0, 0), ("zB", 0, 1, 0, 1), ("wzA", 2, 0, 0), ("wyA", 1, 0, 1), ("wzB", 1, 0, 1), ("zB", 0, 0, 1, 1), ("pa", 1, 0, 0), ("wpT", 1, 0), ("wyA", 1, 0, 2), ("yA", 2, 0, 0), ("pa", 1, 0, 1), ("yA", 0, 0, 2), ("C", 1, 0),),
        (("wzA", 2, 0, 2), ("yA", 2, 0, 2), ("wzA", 2, 0, 1), ("yA", 2, 0, 1), ("wzT", 2, 0), ("S", 1, 0), ("yr", 1, 0, 2), ("TB", 1, 0, 1), ("wzB", 2, 0, 0), ("TB", 1, 0, 0), ("pa", 2, 0, 0), ("wyA", 2, 0, 0), ("yr", 1, 0, 1), ("wyA", 0, 0, 0), ("wyA", 0, 1, 0), ("yr", 1, 0, 0), ("wzB", 2, 0, 1), ("yA", 0, 0, 1), ("wyA", 0, 1, 2), ("wyA", 0, 1, 1), ("wzA", 3, 1, 1), ("wpT", 0, 0), ("wyA", 2, 0, 2), ("paT", 2, 0), ("wyA", 2, 0, 1), ("pa", 2, 0, 1), ("TA", 1, 0, 2), ("yA", 3, 1, 1), ("wpT", 2, 0), ("pa", 0, 1, 0), ("C", 2, 0),),
        (("wzT", 3, 0), ("wzA", 3, 1, 2), ("TA", 1, 0, 1), ("wyA", 0, 0, 2), ("wzA", 3, 1, 0), ("paT", 3, 0), ("TA", 1, 0, 0), ("yA", 3, 1, 0), ("S", 2, 0), ("yA", 3, 1, 2), ("yr", 2, 0, 1), ("wyA", 3, 1, 1), ("wzA", 3, 0, 1), ("wzB", 3, 1, 1), ("yr", 2, 0, 2), ("pa", 0, 0, 0), ("yA", 3, 0, 1), ("TB", 2, 0, 0), ("TB", 2, 0, 1), ("wpT", 3, 0), ("wyA", 0, 0, 1), ("pa", 0, 1, 1), ("wzB", 3, 1, 0), ("pa", 3, 1, 0), ("wyA", 3, 1, 0), ("yr", 2, 0, 0), ("wyA", 3, 1, 2), ("pa", 3, 1, 1), ("wzA", 3, 0, 2), ("TA", 2, 0, 1), ("yA", 3, 0, 2), ("C", 3, 1),),
        (("wzA", 3, 0, 0), ("TA", 2, 0, 2), ("yA", 3, 0, 0), ("TA", 2, 0, 0), ("pa", 0, 0, 1), ("wzB", 3, 0, 0), ("S", 3, 1), ("wzA", 1, 1, 1), ("yr", 3, 1, 0), ("yr", 3, 1, 1), ("yr", 3, 1, 2), ("wyA", 3, 0, 1), ("pa", 3, 0, 0), ("TB", 3, 1, 1), ("yA", 1, 1, 1), ("TB", 3, 1, 0), ("wyA", 3, 0, 2), ("wyA", 3, 0, 0), ("wzB", 3, 0, 1), ("pa", 3, 0, 1), ("wzA", 2, 1, 1), ("yA", 2, 1, 1), ("TA", 3, 1, 0), ("C", 3, 0),),
        (("wzA", 2, 1, 0), ("yA", 2, 1, 0), ("wzA", 2, 1, 2), ("TA", 3, 1, 1), ("TA", 3, 1, 2), ("yA", 2, 1, 2), ("S", 3, 0), ("yr", 3, 0, 1), ("TB", 3, 0, 0), ("yr", 3, 0, 0), ("C", 0, 0),),
        (("TB", 3, 0, 1), ("wyA", 2, 1, 0), ("wzB", 2, 1, 0), ("wyA", 1, 1, 1), ("pa", 2, 1, 0), ("yr", 3, 0, 2), ("wyA", 2, 1, 1), ("wyA", 2, 1, 2), ("wzB", 2, 1, 1), ("pa", 2, 1, 1), ("wzA", 1, 1, 0), ("yA", 1, 1, 0), ("S", 0, 0), ("TA", 3, 0, 0), ("yr", 0, 0, 2), ("TA", 3, 0, 1), ("yr", 0, 0, 0), ("C", 2, 1),),
        (("wzA", 1, 1, 2), ("TA", 3, 0, 2), ("wzB", 1, 1, 0), ("pa", 1, 1, 0), ("yA", 1, 1, 2), ("S", 2, 1), ("yr", 2, 1, 0), ("yr", 2, 1, 1), ("TB", 2, 1, 0), ("C", 0, 1),),
        (("wzB", 1, 1, 1), ("wyA", 1, 1, 0), ("wyA", 1, 1, 2), ("yr", 2, 1, 2), ("TB", 2, 1, 1), ("TA", 2, 1, 0), ("pa", 1, 1, 1), ("yr", 0, 0, 1), ("TA", 2, 1, 1), ("S", 0, 1), ("yr", 0, 1, 1), ("yr", 0, 1, 0), ("C", 1, 1),),
        (("TA", 2, 1, 2), ("FB1", 0, 1), ("S", 1, 1), ("TB", 1, 1, 1), ("yr", 1, 1, 1), ("yr", 1, 1, 0), ("yr", 1, 1, 2), ("TB", 1, 1, 0), ("FB1", 0, 0), ("TA", 1, 1, 1), ("yr", 0, 1, 2), ("TA", 1, 1, 0), ("FB0", 0, 1), ("FA", 0, 0, 1), ("TA", 1, 1, 2), ("FA", 0, 0, 0), ("FB0", 0, 0), ("FA", 0, 0, 2), ("FA", 0, 1, 1), ("FA", 0, 1, 0), ("FA", 0, 1, 2),),
    ),
    (
        (("yA", 1, 0, 0), ("zA", 1, 0, 1, -1), ("zA", 1, 0, 0, -1), ("yT", 1, 0), ("zB", 1, 0, 0, 1), ("zA", 1, 0, 0, 1), ("zA", 1, 0, 1, 1), ("yB", 1, 0), ("zA", 1, 0, 2, -1), ("wyA", 1, 0, 0), ("wyT", 1, 0), ("yB", 1, 1), ("zA", 1, 0, 2, 1), ("zB", 1, 0, 0, -1), ("paT", 1, 0), ("pa", 1, 0, 0), ("wzA", 2, 0, 0), ("zA", 2, 0, 0, -1), ("wzB", 2, 0, 0), ("wzA", 0, 1, 0), ("zT", 1, 0, -1), ("yA", 1, 1, 1), ("zT", 1, 0, 1), ("wzA", 0, 1, 1), ("wzA", 0, 1, 2), ("zA", 0, 1, 0, 1), ("zA", 0, 1, 2, 1), ("wyB", 1, 0), ("wpT", 1, 0), ("zB", 1, 0, 1, 1), ("wzA", 0, 0, 2), ("yA", 1, 0, 1), ("yA", 2, 0, 0), ("zB", 1, 0, 1, -1), ("zB", 2, 0, 0, -1), ("wyA", 1, 0, 1), ("yA", 1, 0, 2), ("wzT", 0, 0), ("wzA", 3, 1, 0), ("wzA", 2, 0, 1), ("wzT", 2, 0), ("wzA", 2, 0, 2), ("zA", 2, 0, 1, -1), ("wzB", 0, 1, 1), ("wzA", 0, 0, 1), ("yA", 2, 0, 2), ("zA", 0, 1, 1, 1), ("zA", 2, 0, 2, -1), ("yA", 2, 0, 1), ("zT", 0, 0, 1), ("yA", 0, 1, 0), ("zA", 0, 0, 1, 1), ("zT", 2, 0, -1), ("yA", 3, 1, 0), ("wzB", 2, 0, 1), ("zA", 0, 0, 2, 1), ("wzA", 3, 1, 2), ("wyB", 1, 1), ("wyA", 2, 0, 2), ("paT", 0, 0), ("wzA", 0, 0, 0), ("yA", 1, 1, 0), ("wzT", 3, 0), ("paT", 2, 0), ("zB", 2, 0, 1, -1), ("wzA", 3, 1, 1), ("zA", 1, 1, 1, 1), ("wyA", 1, 0, 2), ("wzB", 0, 1, 0), ("yA", 3, 1, 1), ("zB", 0, 1, 1, 1), ("pa", 1, 0, 1), ("zA", 3, 1, 1, -1), ("wyA", 2, 0, 0), ("yA", 0, 1, 1), ("zA", 3, 1, 0, -1), ("wzA", 3, 0, 1), ("zB", 0, 1, 0, 1), ("zT", 3, 0, -1), ("zA", 3, 1, 2, -1), ("wyA", 3, 1, 0), ("zA", 3, 0, 1, -1), ("yA", 0, 0, 0), ("paT", 3, 0), ("C", 1, 0),),
        (("wzB", 0, 0, 1), ("yA", 0, 1, 2), ("yA", 3, 0, 1), ("pa", 2, 0, 0), ("wzB", 3, 1, 1), ("zA", 1, 1, 0, 1), ("wpT", 2, 0), ("zA", 0, 0, 0, 1), ("wyA", 1, 1, 1), ("wzB", 0, 0, 0), ("zB", 3, 1, 1, -1), ("wzA", 2, 1, 1), ("yA", 3, 1, 2), ("wyA", 3, 1, 1), ("wzB", 3, 1, 0), ("yA", 0, 0, 1), ("wzA", 3, 0, 2), ("wyA", 2, 0, 1), ("pa", 2, 0, 1), ("zB", 0, 0, 0, 1), ("zB", 3, 1, 0, -1), ("yA", 0, 0, 2), ("C", 2, 0),),
        (("zB", 0, 0, 1, 1), ("zA", 1, 1, 2, 1), ("wyA", 0, 1, 1), ("wzA", 2, 1, 0), ("zA", 3, 0, 2, -1), ("wyA", 3, 1, 2), ("wyA", 0, 1, 0), ("wzA", 3, 0, 0), ("zA", 3, 0, 0, -1), ("pa", 0, 1, 0), ("yA", 3, 0, 2), ("wyA", 0, 0, 1), ("yA", 2, 1, 0), ("S", 1, 0), ("wzB", 3, 0, 0), ("S", 2, 0), ("pa", 3, 1, 1), ("pa", 3, 1, 0), ("wyA", 0, 0, 2), ("pa", 1, 1, 0), ("wyA", 0, 1, 2), ("wyA", 0, 0, 0), ("zB", 3, 0, 0, -1), ("zB", 1, 1, 1, 1), ("yr", 2, 0, 2), ("yr", 2, 0, 1), ("yA", 1, 1, 2), ("wzB", 3, 0, 1), ("zA", 1, 1, 1, -1), ("wpT", 3, 0), ("yA", 2, 1, 1), ("yA", 3, 0, 0), ("pa", 0, 0, 0), ("zB", 1, 1, 0, 1), ("zB", 3, 0, 1, -1), ("zA", 2, 1, 1, -1), ("pa", 0, 1, 1), ("wpT", 0, 0), ("C", 3, 1),),
        (("wzA", 2, 1, 2), ("TB", 2, 0, 1), ("TA", 2, 0, 1), ("wyA", 3, 0, 1), ("TB", 2, 0, 0), ("yr", 1, 0, 1), ("TA", 2, 0, 2), ("zA", 2, 1, 0, -1), ("zA", 2, 1, 2, -1), ("pa", 0, 0, 1), ("yr", 2, 0, 0), ("wzB", 2, 1, 1), ("zB", 2, 1, 1, -1), ("C", 0, 1),),
        (("wzB", 2, 1, 0), ("zB", 2, 1, 0, -1), ("wyA", 3, 0, 0), ("yA", 2, 1, 2), ("S", 3, 1), ("yr", 3, 1, 2), ("wyA", 1, 1, 2), ("wyA", 1, 1, 0), ("pa", 3, 0, 0), ("wyA", 2, 1, 0), ("zA", 1, 1, 0, -1), ("yr", 3, 1, 0), ("C", 0, 0),),
        (("zA", 1, 1, 2, -1), ("S", 0, 1), ("zB", 1, 1, 0, -1), ("yr", 0, 1, 0), ("wyA", 3, 0, 2), ("TB", 3, 1, 0), ("wyA", 2, 1, 1), ("FA", 1, 0, 1), ("wyA", 2, 1, 2), ("pa", 3, 0, 1), ("FB1", 1, 0), ("yr", 3, 1, 1), ("TB", 3, 1, 1), ("yr", 0, 1, 2), ("C", 3, 0),),
        (("zB", 1, 1, 1, -1), ("pa", 2, 1, 1), ("pa", 1, 1, 1), ("yr", 0, 1, 1), ("S", 0, 0), ("TA", 3, 1, 0), ("S", 3, 0), ("TB", 0, 1, 0), ("pa", 2, 1, 0), ("TA", 2, 0, 0), ("yr", 3, 0, 2), ("yr", 3, 0, 1), ("TA", 3, 1, 2), ("TB", 0, 1, 1), ("TB", 3, 0, 0), ("TA", 3, 1, 1), ("C", 2, 1),),
        (("TB", 3, 0, 1), ("TA", 0, 1, 0), ("yr", 0, 0, 1), ("yr", 1, 0, 0), ("C", 1, 1),),
        (("TA", 3, 0, 1), ("yr", 0, 0, 0), ("S", 2, 1), ("TB", 0, 0, 0), ("yr", 2, 1, 0), ("S", 1, 1), ("yr", 1, 0, 2), ("TB", 0, 0, 1), ("yr", 3, 0, 0), ("TA", 3, 0, 2), ("TB", 2, 1, 1), ("TA", 0, 0, 1), ("yr", 2, 1, 2), ("yr", 0, 0, 2), ("yr", 2, 1, 1), ("TA", 2, 1, 0), ("FB0", 1, 0), ("TA", 3, 0, 0), ("yr", 1, 1, 0), ("FA", 1, 0, 0), ("TB", 2, 1, 0), ("yr", 1, 1, 1), ("TA", 0, 1, 1), ("TA", 0, 0, 2), ("TA", 2, 1, 1), ("FB1", 1, 1), ("TA", 0, 1, 2), ("TA", 2, 1, 2), ("TA", 0, 0, 0), ("yr", 1, 1, 2), ("FA", 1, 1, 0), ("FA", 1, 1, 1), ("FA", 1, 0, 2), ("FB0", 1, 1), ("FA", 1, 1, 2),),
    ),
)


def chunk_of(size, most=1024):
    chunk = most
    while size % chunk:
        chunk -= LANES
    return chunk


def expert_weights(gate_ids, gate_values, columns):
    expert_row = jnp.arange(columns, dtype=jnp.int32)
    return jnp.sum(
        jnp.where(
            gate_ids[:, :, None] == expert_row[None, None, :],
            gate_values.astype(jnp.float32)[:, :, None],
            jnp.float32(0.0),
        ),
        axis=1,
    ).astype(jnp.bfloat16)


def single_columns(width):
    return max(LANES, width * SINGLE[0] // (SINGLE[1] * LANES) * LANES)


def tree_kernel(
    tokens, ids_hbm, values_hbm, wg_hbm, wu_hbm, wd_hbm, out,
    ids, values, tables, x, wg, wu, wd, pin, pout, own, rs_a, rs_b, yr_a, yr_b,
    gate_sem, weight_sem, own_sem, za_send, za_recv, zb_send, zb_recv, ya_send, ya_recv, yb_send, yb_recv,
    yt_send, yt_recv, zt_send, zt_recv, pat_send, pat_recv,
    pa_send, pa_recv, pp_send, pp_recv, ra_send, ra_recv, rb_send, rb_recv,
    yra_send, yra_recv, yrb_send, yrb_recv,
):
    tok, width = tokens.shape
    wa = single_columns(width)
    rows = tok // SLICES
    node = lax.axis_index("node")
    other_core = {"local": 1 - lax.axis_index("local")}
    plane, column = node // COLUMNS, node % COLUMNS
    across = {"node": node + 1 - 2 * column}
    flip = jnp.where(plane >= PLANES // 2, 1, 0)
    near = plane * (1 - flip) + (PLANES - 1 - plane) * flip

    def actual(t):
        return t * (1 - flip) + (PLANES - 1 - t) * flip

    def along(s):
        return {"node": node + COLUMNS * s * (1 - 2 * flip)}

    def upward(s):
        return (1 - flip) if s > 0 else flip

    cols_b = pl.ds(wa, width - wa)
    bounds = [wa // LANES * j // PIECES * LANES for j in range(PIECES + 1)]
    cols_a = [pl.ds(bounds[j], bounds[j + 1] - bounds[j]) for j in range(PIECES)]

    keeps = [
        pltpu.make_async_copy(
            tokens.at[pl.ds(h * rows, rows)],
            x.at[plane, h, pl.ds(0, rows)],
            own_sem.at[h],
        )
        for h in range(SLICES)
    ]
    gates = [
        pltpu.make_async_copy(src, dst, gate_sem.at[k])
        for k, (src, dst) in enumerate(((ids_hbm, ids), (values_hbm, values)))
    ]
    for keep in keeps + gates:
        keep.start()
    loads = [
        pltpu.make_async_copy(src, dst, weight_sem.at[k])
        for k, (src, dst) in enumerate(((wg_hbm, wg), (wu_hbm, wu), (wd_hbm, wd)))
    ]

    barrier = pltpu.get_barrier_semaphore()
    for target in (other_core, across, along(1)):
        pl.semaphore_signal(barrier, inc=1, device_id=target, device_id_type=MESH)

    @pl.when(near > 0)
    def _():
        pl.semaphore_signal(barrier, inc=1, device_id=along(-1), device_id_type=MESH)

    pl.semaphore_wait(barrier, 3 + jnp.where(near > 0, 1, 0))
    for keep in keeps:
        keep.wait()
    for load in loads:
        load.start()

    first, second = pl.ds(0, rows), pl.ds(rows, rows)
    part = (first, second)

    def copy(src, dst, send, recv, target):
        return pltpu.make_async_remote_copy(
            src_ref=src, dst_ref=dst, send_sem=send, recv_sem=recv,
            device_id=target, device_id_type=MESH,
        )

    def fill_table():
        for gate in gates:
            gate.wait()
        table_row = lax.broadcasted_iota(jnp.int32, (tables.shape[3], tok), 0)
        table = jnp.zeros(table_row.shape, jnp.float32)
        for choice in range(ids.shape[0]):
            chosen = table_row == ids[pl.ds(choice, 1), :]
            weight = values[pl.ds(choice, 1), :].astype(jnp.float32)
            table += jnp.where(chosen, weight, 0.0)
        tables[plane, 0, 0, :, pl.ds(0, tok)] = table.astype(jnp.bfloat16)

    def sums(t, s):
        up = upward(s)
        return up, actual(t) - up

    def send(op):
        kind, t, h = op[:3]
        p = actual(t)
        if kind == "zA":
            j, s = op[3:]
            ref = x.at[p, h, first, cols_a[j]]
            return copy(ref, ref, za_send.at[max(s, 0), p, h, j], za_recv.at[p, h, j], along(s))
        if kind == "zB":
            j, s = op[3:]
            ref = x.at[p, h, part[j], cols_b]
            return copy(ref, ref, zb_send.at[max(s, 0), p, h, j], zb_recv.at[p, h, j], along(s))
        if kind == "yA":
            j = op[3]
            return copy(
                x.at[p, h, first, cols_a[j]], x.at[p, h, second, cols_a[j]],
                ya_send.at[p, h, j], ya_recv.at[p, h, j], across,
            )
        if kind == "yB":
            return copy(
                x.at[p, h, first, cols_b], x.at[p, h, second, cols_b],
                yb_send.at[h], yb_recv.at[h], across,
            )
        if kind == "yT":
            return copy(tables.at[p, 0, 0], tables.at[p, 0, 1], yt_send.at[0], yt_recv.at[0], across)
        if kind == "zT":
            s = op[3]
            ref = tables.at[p, 0]
            return copy(ref, ref, zt_send.at[max(s, 0), p], zt_recv.at[p], along(s))
        if kind == "paT":
            return copy(
                tables.at[p, 0], tables.at[p, 1], pat_send.at[p], pat_recv.at[p], other_core
            )
        if kind == "pa":
            return copy(
                x.at[p, h, part[op[3]]], x.at[p, h, pl.ds((2 + op[3]) * rows, rows)],
                pa_send.at[p, h, op[3]], pa_recv.at[p, h, op[3]], other_core,
            )
        if kind == "yr":
            j = op[3]
            return copy(
                pin.at[p, h, second, cols_a[j]], yr_a.at[p, h, :, cols_a[j]],
                yra_send.at[p, h, j], yra_recv.at[p, h, j], across,
            )
        if kind == "FB1":
            return copy(
                pin.at[p, h, second, cols_b], yr_b.at[h], yrb_send.at[h], yrb_recv.at[h], across
            )
        j, s = op[3:]
        up, place = sums(t, s)
        if kind == "TA":
            return copy(
                pin.at[p, h, first, cols_a[j]], rs_a.at[up, place, h, :, cols_a[j]],
                ra_send.at[p, h, j], ra_recv.at[up, p, h, j], along(s),
            )
        return copy(
            pin.at[p, h, part[j], cols_b], rs_b.at[up, place, h, part[j]],
            rb_send.at[p, h, j], rb_recv.at[up, p, h, j], along(s),
        )

    def pp(p, h, slot):
        return copy(pout.at[slot], pin.at[p, h], pp_send.at[slot], pp_recv.at[p, h], other_core)

    def add_up(dst, terms, size):
        step = chunk_of(size, 2304)

        @pl.loop(0, size // step)
        def _(k):
            at = pl.multiple_of(k * step, LANES)
            total = terms[0](at, step).astype(jnp.float32)
            for term in terms[1:]:
                total += term(at, step).astype(jnp.float32)
            dst(at, step, total.astype(jnp.bfloat16))

    def run(op, z, slot_of):
        kind, t, h = op[:3]
        p = actual(t)
        towards = 1 if t > z else -1
        sides = [s for s in (1, -1) if 0 <= z + s < PLANES]
        if kind in ("zA", "zB", "zT", "yA", "yB", "yT", "pa", "paT", "yr"):
            send(op).start()
        elif kind == "wzT":
            send(("zT", t, h, 1)).wait_recv()
        elif kind == "wyT":
            send(("yT", t, h)).wait_recv()
        elif kind == "wpT":
            send(("paT", t, h)).wait_recv()
        elif kind == "wzA":
            send(("zA", t, h, op[3], 1)).wait_recv()
        elif kind == "wzB":
            send(("zB", t, h, op[3], 1)).wait_recv()
        elif kind == "wyA":
            send(("yA", *op[1:])).wait_recv()
        elif kind == "wyB":
            send(("yB", t, h)).wait_recv()
        elif kind == "S":
            slot = slot_of[(t, h)]
            pp(p, h, slot).wait_recv()

            def joined(at, step, value):
                pin[p, h, :, pl.ds(at, step)] = value

            add_up(
                joined,
                (
                    lambda at, step: own[slot, :, pl.ds(at, step)],
                    lambda at, step: pin[p, h, :, pl.ds(at, step)],
                ),
                width,
            )
        elif kind == "TB":
            j = op[3]
            if 0 <= z - towards < PLANES:
                up, place = sums(t, towards)
                send((*op, towards)).wait_recv()

                def passed(at, step, value):
                    pin[p, h, part[j], pl.ds(wa + at, step)] = value

                add_up(
                    passed,
                    (
                        lambda at, step: pin[p, h, part[j], pl.ds(wa + at, step)],
                        lambda at, step: rs_b[up, place, h, part[j], pl.ds(at, step)],
                    ),
                    width - wa,
                )
            send((*op, towards)).start()
        elif kind in ("TA", "FA"):
            j = op[3]
            send(("yr", *op[1:])).wait_recv()
            terms = [
                lambda at, step: pin[p, h, first, pl.ds(bounds[j] + at, step)],
                lambda at, step: yr_a[p, h, :, pl.ds(bounds[j] + at, step)],
            ]
            own_plane = kind == "FA"
            for s in [-s for s in sides] if own_plane else [towards]:
                if own_plane or 0 <= z - towards < PLANES:
                    up, place = sums(t, s)
                    send(("TA", t, h, j, s)).wait_recv()
                    terms.append(
                        lambda at, step, up=up, place=place: rs_a[
                            up, place, h, :, pl.ds(bounds[j] + at, step)
                        ]
                    )

            def finished(at, step, value):
                if own_plane:
                    out[pl.ds(h * rows, rows), pl.ds(bounds[j] + at, step)] = value
                else:
                    pin[p, h, first, pl.ds(bounds[j] + at, step)] = value

            add_up(finished, terms, bounds[j + 1] - bounds[j])
            if not own_plane:
                send((*op, towards)).start()
        elif kind in ("FB0", "FB1"):
            j = int(kind == "FB1")
            terms = [lambda at, step: pin[p, h, part[j], pl.ds(wa + at, step)]]
            if j == 0:
                send(("FB1", t, h)).wait_recv()
                terms.append(lambda at, step: yr_b[h, :, pl.ds(at, step)])
            for s in sides:
                up, place = sums(t, -s)
                send(("TB", t, h, j, -s)).wait_recv()
                terms.append(
                    lambda at, step, up=up, place=place: rs_b[
                        up, place, h, part[j], pl.ds(at, step)
                    ]
                )

            def settled(at, step, value):
                if j == 0:
                    out[pl.ds(h * rows, rows), pl.ds(wa + at, step)] = value
                else:
                    pin[p, h, second, pl.ds(wa + at, step)] = value

            add_up(settled, terms, width - wa)
            if j == 1:
                send(op).start()

    def compute(k, p, h):
        slot = k % 2
        for side in range(2):
            copy(
                x.at[p, h, pl.ds(side * rows, rows)], x.at[p, h, pl.ds((2 + side) * rows, rows)],
                pa_send.at[p, h, side], pa_recv.at[p, h, side], other_core,
            ).wait_recv()

        @pl.when(k == 0)
        def _():
            loads[0].wait()
            loads[1].wait()

        @pl.when(k >= 2)
        def _():
            pp(p, h, slot).wait_send()

        gate = jnp.dot(x[p, h], wg[...], preferred_element_type=jnp.float32)
        up = jnp.dot(x[p, h], wu[...], preferred_element_type=jnp.float32)
        hidden = (gate / (1.0 + jnp.exp(-gate)) * up).astype(jnp.bfloat16)
        expert = lax.broadcasted_iota(jnp.int32, tables.shape[3:], 0) == node
        token = lax.broadcasted_iota(jnp.int32, (rows, LANES), 1) == (
            lax.broadcasted_iota(jnp.int32, (rows, LANES), 0) + h * rows
        )
        weights = []
        for core in range(2):
            for side in range(COLUMNS):
                table = tables[p, core, side].astype(jnp.float32)
                row = jnp.sum(jnp.where(expert, table, 0.0), axis=0, keepdims=True)
                weights.append(jnp.sum(jnp.where(token, row, 0.0), axis=1, keepdims=True))
        scale = jnp.concatenate(weights, axis=0)

        @pl.when(k == 0)
        def _():
            loads[2].wait()

        step = chunk_of(width, 1792)
        for c in range(width // step):
            cols = pl.ds(c * step, step)
            value = jnp.dot(hidden, wd[:, cols], preferred_element_type=jnp.float32) * scale
            own[slot, :, cols] = value[:2 * rows]
            pout[slot, :, cols] = value[2 * rows:].astype(jnp.bfloat16)
        pp(p, h, slot).start()

    items = [[group[-1][1:3] for group in groups[:-1]] for groups in SCHEDULE]
    count = len(items[0])

    @pl.loop(0, count)
    def _(k):
        for z, groups in enumerate(SCHEDULE):
            slot_of = {item: i % 2 for i, item in enumerate(items[z])}
            tabled = [
                op for op in groups[0]
                if op[0] == "yT"
            ]
            for i, group in enumerate(groups[:-1]):

                @pl.when((near == z) & (k == i))
                def _(group=group, z=z, slot_of=slot_of, at=tabled[0] if i == 0 else None):
                    for op in group[:-1]:
                        if op == at:
                            fill_table()
                        run(op, z, slot_of)

        t, h = 0, 0
        for z, of in enumerate(items):
            for i, item in enumerate(of):
                here = jnp.where(near == z, 1, 0) * jnp.where(k == i, 1, 0)
                t, h = t + here * item[0], h + here * item[1]
        compute(k, actual(t), h)

    for z, groups in enumerate(SCHEDULE):
        slot_of = {item: i % 2 for i, item in enumerate(items[z])}

        @pl.when(near == z)
        def _(groups=groups, z=z, slot_of=slot_of):
            for op in groups[-1]:
                run(op, z, slot_of)
            for group in groups:
                for op in group:
                    if op[0] in ("zA", "zB", "zT", "yA", "yB", "yT", "pa", "paT", "yr", "FB1"):
                        send(op).wait_send()
                    elif op[0] in ("TA", "TB"):
                        send((*op, 1 if op[1] > z else -1)).wait_send()
            for t, h in items[z][-2:]:
                pp(actual(t), h, slot_of[(t, h)]).wait_send()


def buffers(tok, width, hid, topk):
    wa = single_columns(width)
    rows = tok // SLICES
    kind = jnp.bfloat16
    return [
        pltpu.VMEM((topk, tok), jnp.int32),
        pltpu.VMEM((topk, tok), kind),
        pltpu.VMEM((PLANES, 2, COLUMNS, 16, LANES), kind),
        pltpu.VMEM((PLANES, SLICES, 4 * rows, width), kind),
        pltpu.VMEM((width, hid), kind),
        pltpu.VMEM((width, hid), kind),
        pltpu.VMEM((hid, width), kind),
        pltpu.VMEM((PLANES, SLICES, 2 * rows, width), kind),
        pltpu.VMEM((2, 2 * rows, width), kind),
        pltpu.VMEM((2, 2 * rows, width), jnp.float32),
        pltpu.VMEM((2, PLANES - 1, SLICES, rows, wa), kind),
        pltpu.VMEM((2, PLANES - 1, SLICES, 2 * rows, width - wa), kind),
        pltpu.VMEM((PLANES, SLICES, rows, wa), kind),
        pltpu.VMEM((SLICES, rows, width - wa), kind),
    ]


def by_trees(tokens, gate_ids, gate_values, w_gate, w_up, w_down):
    tok, width = tokens.shape
    anywhere = pl.BlockSpec(memory_space=pl.ANY)
    in_vmem = pl.BlockSpec(memory_space=pltpu.VMEM)

    def dma(*shape):
        return pltpu.SemaphoreType.DMA(shape)

    each = (PLANES, SLICES)
    return pl.pallas_call(
        tree_kernel,
        out_shape=jax.ShapeDtypeStruct((tok, width), jnp.bfloat16),
        in_specs=[anywhere] * 6,
        out_specs=in_vmem,
        scratch_shapes=[
            *buffers(tok, width, w_gate.shape[2], gate_ids.shape[1]),
            dma(2), dma(3), dma(SLICES),
            dma(2, *each, PIECES), dma(*each, PIECES), dma(2, *each, 2), dma(*each, 2),
            dma(*each, PIECES), dma(*each, PIECES), dma(SLICES), dma(SLICES),
            dma(1), dma(1), dma(2, PLANES), dma(PLANES), dma(PLANES), dma(PLANES),
            dma(*each, 2), dma(*each, 2), dma(2), dma(*each),
            dma(*each, PIECES), dma(2, *each, PIECES), dma(*each, 2), dma(2, *each, 2),
            dma(*each, PIECES), dma(*each, PIECES), dma(SLICES), dma(SLICES),
        ],
        compiler_params=pltpu.CompilerParams(
            collective_id=0, has_side_effects=True, vmem_limit_bytes=VMEM_LIMIT
        ),
    )(tokens, gate_ids.T, gate_values.T, w_gate[0], w_up[0], w_down[0])


def by_collectives(tokens, gate_ids, gate_values, w_gate, w_up, w_down):
    n = lax.axis_size("node")
    every = ("node", "local")
    weights = lax.all_gather(expert_weights(gate_ids, gate_values, n), every, axis=0, tiled=True)
    rows = lax.all_gather(tokens, every, axis=0, tiled=True)
    mine = (jnp.arange(n, dtype=jnp.int32) == lax.axis_index("node"))[None, :]
    scale = jnp.sum(jnp.where(mine, weights.astype(jnp.float32), 0.0), axis=1, keepdims=True)
    gate_act = jnp.dot(rows, w_gate[0], preferred_element_type=jnp.float32)
    up_act = jnp.dot(rows, w_up[0], preferred_element_type=jnp.float32)
    hidden = (jax.nn.silu(gate_act) * up_act).astype(jnp.bfloat16)
    partial_value = jnp.dot(hidden, w_down[0], preferred_element_type=jnp.float32) * scale
    return lax.psum_scatter(
        partial_value.astype(jnp.bfloat16), every, scatter_dimension=0, tiled=True
    )


def trees_fit(n, tok, width, hid, topk):
    if n != PLANES * COLUMNS or lax.axis_size("local") != 2 or tok % (16 * SLICES) or width % LANES:
        return False
    if width < 2 * LANES or tok > LANES or n > 16:
        return False
    size = 2 * tok * width + 2**21
    for ref in buffers(tok, width, hid, topk):
        size += ref.inner_aval.size * ref.inner_aval.dtype.itemsize
    return size < VMEM_LIMIT


def per_device(tokens, gate_ids, gate_values, w_gate, w_up, w_down):
    n = lax.axis_size("node")
    args = (tokens, gate_ids, gate_values, w_gate, w_up, w_down)
    if trees_fit(n, *tokens.shape, w_gate.shape[2], gate_ids.shape[1]):
        return by_trees(*args)
    return by_collectives(*args)


def solution(mesh):
    return jax.shard_map(
        per_device,
        mesh=mesh,
        in_specs=(
            P(("rep", "node", "local"), None),
            P(("rep", "node", "local"), None),
            P(("rep", "node", "local"), None),
            P("node", None, "local"),
            P("node", None, "local"),
            P("node", "local", None),
        ),
        out_specs=P(("rep", "node", "local"), None),
        check_vma=False,
    )
```

```python
import functools

import jax
import jax.numpy as jnp
from jax import lax
from jax.experimental import pallas as pl
from jax.experimental.pallas import tpu as pltpu
from jax.sharding import PartitionSpec as P

MESH = pl.DeviceIdType.MESH
LANES = 128
VMEM_LIMIT = 67_000_000
PLANES = 4
COLUMNS = 2
SLICES = 2
SINGLE = (34, 33)
SINGLE_OF = 56
PIECES = 2

SCHEDULE = (
    (
        (("zA", 0, 0, 1, 1), ("yB", 0, 0), ("zA", 0, 1, 1, 1), ("yA", 0, 0, 1), ("wzA", 1, 1, 1), ("zA", 0, 1, 0, 1), ("yT", 0, 0), ("zA", 0, 0, 0, 1), ("yA", 1, 1, 1), ("wzA", 1, 1, 0), ("zB", 0, 0, 0, 1), ("wyB", 0, 0), ("yA", 0, 0, 0), ("yA", 1, 1, 0), ("wyA", 1, 1, 1), ("wyT", 0, 0), ("yB", 0, 1), ("zT", 0, 0, 1), ("zB", 0, 0, 1, 1), ("yA", 0, 1, 0), ("wzT", 1, 0), ("zB", 0, 1, 0, 1), ("wzB", 1, 1, 0), ("pa", 1, 1, 0), ("wzB", 1, 1, 1), ("wyA", 1, 1, 0), ("paT", 1, 0), ("wzT", 2, 0), ("pa", 1, 1, 1), ("wpT", 1, 0), ("wzA", 2, 1, 0), ("yA", 2, 1, 0), ("C", 1, 1),),
        (("wyB", 0, 1), ("wzA", 2, 1, 1), ("zB", 0, 1, 1, 1), ("yA", 2, 1, 1), ("S", 1, 1), ("yr", 1, 1, 0), ("paT", 2, 0), ("TB", 1, 1, 0), ("wzB", 2, 1, 0), ("TB", 1, 1, 1), ("wyA", 2, 1, 0), ("pa", 2, 1, 0), ("wzB", 2, 1, 1), ("yr", 1, 1, 1), ("wyA", 2, 1, 1), ("pa", 2, 1, 1), ("wpT", 2, 0), ("wyA", 0, 0, 1), ("wzA", 3, 0, 0), ("paT", 0, 0), ("yA", 3, 0, 0), ("TA", 1, 1, 0), ("C", 2, 1),),
        (("wyA", 0, 0, 0), ("wzA", 3, 0, 1), ("yA", 3, 0, 1), ("TA", 1, 1, 1), ("S", 2, 1), ("yr", 2, 1, 1), ("TB", 2, 1, 0), ("pa", 0, 0, 1), ("yr", 2, 1, 0), ("yA", 0, 1, 1), ("wzT", 3, 0), ("wzB", 3, 0, 0), ("paT", 3, 0), ("wpT", 3, 0), ("wzB", 3, 0, 1), ("wyA", 3, 0, 0), ("pa", 3, 0, 0), ("wyA", 3, 0, 1), ("TB", 2, 1, 1), ("pa", 0, 0, 0), ("pa", 3, 0, 1), ("TA", 2, 1, 1), ("wzA", 3, 1, 1), ("yA", 3, 1, 1), ("C", 3, 0),),
        (("wpT", 0, 0), ("wzA", 3, 1, 0), ("yA", 3, 1, 0), ("wyA", 0, 1, 1), ("TA", 2, 1, 0), ("S", 3, 0), ("TB", 3, 0, 1), ("pa", 0, 1, 0), ("yr", 3, 0, 1), ("wzB", 3, 1, 0), ("pa", 3, 1, 0), ("yr", 3, 0, 0), ("C", 0, 0),),
        (("wyA", 3, 1, 0), ("wyA", 3, 1, 1), ("wzB", 3, 1, 1), ("TB", 3, 0, 0), ("pa", 3, 1, 1), ("wzA", 2, 0, 0), ("yA", 2, 0, 0), ("S", 0, 0), ("TA", 3, 0, 1), ("yr", 0, 0, 1), ("C", 3, 1),),
        (("wzA", 2, 0, 1), ("yA", 2, 0, 1), ("wyA", 0, 1, 0), ("TA", 3, 0, 0), ("S", 3, 1), ("wzB", 2, 0, 0), ("TB", 3, 1, 1), ("yr", 3, 1, 1), ("wyA", 2, 0, 0), ("wzB", 2, 0, 1), ("wyA", 2, 0, 1), ("pa", 2, 0, 1), ("yr", 3, 1, 0), ("pa", 2, 0, 0), ("TB", 3, 1, 0), ("wzA", 1, 0, 0), ("yA", 1, 0, 0), ("TA", 3, 1, 1), ("C", 2, 0),),
        (("pa", 0, 1, 1), ("wzA", 1, 0, 1), ("yA", 1, 0, 1), ("TA", 3, 1, 0), ("S", 2, 0), ("yr", 2, 0, 1), ("yr", 0, 0, 0), ("TB", 2, 0, 1), ("TB", 2, 0, 0), ("wzB", 1, 0, 0), ("pa", 1, 0, 0), ("C", 0, 1),),
        (("wyA", 1, 0, 0), ("wyA", 1, 0, 1), ("wzB", 1, 0, 1), ("pa", 1, 0, 1), ("yr", 2, 0, 0), ("S", 0, 1), ("TA", 2, 0, 1), ("yr", 0, 1, 0), ("C", 1, 0),),
        (("TA", 2, 0, 0), ("yr", 0, 1, 1), ("S", 1, 0), ("TB", 1, 0, 1), ("TB", 1, 0, 0), ("yr", 1, 0, 1), ("yr", 1, 0, 0), ("FB1", 0, 0), ("FB1", 0, 1), ("FA", 0, 1, 1), ("TA", 1, 0, 1), ("FA", 0, 0, 0), ("FA", 0, 0, 1), ("TA", 1, 0, 0), ("FB0", 0, 0), ("FA", 0, 1, 0), ("FB0", 0, 1),),
    ),
    (
        (("zA", 1, 1, 1, -1), ("zA", 1, 1, 0, -1), ("zA", 1, 1, 1, 1), ("yT", 1, 0), ("yB", 1, 1), ("zB", 1, 1, 0, 1), ("yA", 1, 1, 1), ("zB", 1, 1, 0, -1), ("wyB", 1, 1), ("zA", 1, 1, 0, 1), ("wyT", 1, 0), ("wzA", 2, 1, 1), ("yB", 1, 0), ("yA", 1, 1, 0), ("zT", 1, 0, 1), ("wzA", 0, 0, 1), ("zB", 1, 1, 1, 1), ("zT", 1, 0, -1), ("zB", 1, 1, 1, -1), ("wzA", 2, 1, 0), ("wzT", 2, 0), ("wzA", 0, 0, 0), ("zT", 2, 0, -1), ("yA", 0, 0, 1), ("zA", 0, 0, 0, 1), ("zA", 2, 1, 0, -1), ("paT", 1, 0), ("wyA", 1, 1, 0), ("pa", 1, 0, 0), ("wzB", 2, 1, 1), ("zA", 2, 1, 1, -1), ("wzA", 0, 1, 1), ("yA", 2, 1, 0), ("zA", 0, 0, 1, 1), ("wzT", 0, 0), ("wyA", 1, 1, 1), ("zT", 0, 0, 1), ("pa", 1, 1, 1), ("yA", 0, 0, 0), ("wzB", 2, 1, 0), ("wzA", 3, 0, 0), ("yA", 2, 1, 1), ("zA", 0, 1, 1, 1), ("zB", 2, 1, 1, -1), ("zB", 2, 1, 0, -1), ("wpT", 1, 0), ("paT", 0, 0), ("wzT", 3, 0), ("wzB", 0, 0, 0), ("wzA", 3, 0, 1), ("wzB", 0, 0, 1), ("wzA", 0, 1, 0), ("yA", 0, 1, 1), ("zB", 0, 0, 0, 1), ("zA", 3, 0, 0, -1), ("zA", 3, 0, 1, -1), ("pa", 1, 1, 0), ("zT", 3, 0, -1), ("paT", 2, 0), ("wpT", 0, 0), ("yA", 3, 0, 1), ("zB", 0, 0, 1, 1), ("C", 1, 1),),
        (("pa", 2, 1, 0), ("wzA", 3, 1, 1), ("zA", 0, 1, 0, 1), ("wyA", 2, 1, 1), ("wzB", 0, 1, 0), ("zB", 0, 1, 0, 1), ("wyA", 2, 1, 0), ("wyA", 0, 0, 0), ("wyA", 0, 1, 1), ("pa", 0, 1, 0), ("pa", 2, 1, 1), ("yA", 0, 1, 0), ("wpT", 2, 0), ("zA", 1, 0, 0, 1), ("yA", 1, 0, 0), ("S", 1, 1), ("wzB", 3, 0, 1), ("yA", 3, 0, 0), ("wzB", 3, 0, 0), ("wzB", 0, 1, 1), ("zB", 3, 0, 0, -1), ("zB", 3, 0, 1, -1), ("paT", 3, 0), ("pa", 0, 0, 0), ("C", 2, 1),),
        (("wzA", 3, 1, 0), ("yA", 1, 0, 1), ("zB", 0, 1, 1, 1), ("wyA", 0, 1, 0), ("wzB", 3, 1, 0), ("wpT", 3, 0), ("wyB", 1, 0), ("zA", 3, 1, 1, -1), ("yA", 3, 1, 0), ("pa", 3, 1, 0), ("pa", 3, 0, 0), ("wyA", 3, 0, 0), ("yr", 1, 1, 1), ("wyA", 3, 0, 1), ("pa", 3, 0, 1), ("wzA", 2, 0, 0), ("wyA", 0, 0, 1), ("pa", 0, 0, 1), ("zA", 3, 1, 0, -1), ("zB", 1, 0, 0, 1), ("S", 2, 1), ("yA", 2, 0, 0), ("zA", 1, 0, 1, 1), ("yA", 3, 1, 1), ("wzB", 3, 1, 1), ("zB", 3, 1, 0, -1), ("pa", 0, 1, 1), ("C", 3, 0),),
        (("zB", 3, 1, 1, -1), ("yr", 2, 1, 1), ("zA", 2, 0, 0, -1), ("wyA", 3, 1, 0), ("zB", 1, 0, 1, 1), ("C", 0, 0),),
        (("wzB", 2, 0, 0), ("TB", 2, 1, 1), ("wyA", 2, 0, 0), ("wzA", 2, 0, 1), ("yr", 2, 1, 0), ("S", 3, 0), ("wyA", 1, 0, 1), ("wyA", 3, 1, 1), ("zA", 2, 0, 1, -1), ("yA", 2, 0, 1), ("yr", 1, 1, 0), ("wzB", 2, 0, 1), ("zB", 2, 0, 0, -1), ("TB", 2, 1, 0), ("C", 0, 1),),
        (("TA", 2, 1, 0), ("wyA", 1, 0, 0), ("pa", 3, 1, 1), ("S", 0, 0), ("zB", 2, 0, 1, -1), ("yr", 3, 0, 1), ("pa", 2, 0, 0), ("zA", 1, 0, 0, -1), ("TB", 3, 0, 0), ("S", 0, 1), ("pa", 1, 0, 1), ("C", 3, 1),),
        (("zA", 1, 0, 1, -1), ("yr", 3, 0, 0), ("zB", 1, 0, 0, -1), ("yr", 0, 0, 1), ("FA", 1, 1, 0), ("wyA", 2, 0, 1), ("TB", 3, 0, 1), ("S", 3, 1), ("yr", 3, 1, 1), ("FB1", 1, 1), ("yr", 0, 1, 0), ("pa", 2, 0, 1), ("yr", 0, 1, 1), ("TA", 3, 0, 1), ("TB", 3, 1, 1), ("zB", 1, 0, 1, -1), ("C", 2, 0),),
        (("yr", 3, 1, 0), ("TB", 0, 0, 1), ("TA", 3, 0, 0), ("TA", 0, 0, 1), ("yr", 0, 0, 0), ("TA", 3, 1, 1), ("TB", 0, 0, 0), ("TA", 2, 1, 1), ("TB", 3, 1, 0), ("S", 2, 0), ("yr", 2, 0, 1), ("C", 1, 0),),
        (("TA", 0, 1, 1), ("S", 1, 0), ("TA", 3, 1, 0), ("TB", 2, 0, 1), ("FB0", 1, 1), ("TB", 2, 0, 0), ("yr", 2, 0, 0), ("TB", 0, 1, 1), ("TA", 0, 0, 0), ("TA", 0, 1, 0), ("yr", 1, 0, 0), ("yr", 1, 0, 1), ("TA", 2, 0, 1), ("TA", 2, 0, 0), ("FB1", 1, 0), ("TB", 0, 1, 0), ("FA", 1, 0, 1), ("FB0", 1, 0), ("FA", 1, 1, 1), ("FA", 1, 0, 0),),
    ),
)


def chunk_of(size, most=1024):
    chunk = most
    while size % chunk:
        chunk -= LANES
    return chunk


def expert_weights(gate_ids, gate_values, columns):
    expert_row = jnp.arange(columns, dtype=jnp.int32)
    return jnp.sum(
        jnp.where(
            gate_ids[:, :, None] == expert_row[None, None, :],
            gate_values.astype(jnp.float32)[:, :, None],
            jnp.float32(0.0),
        ),
        axis=1,
    ).astype(jnp.bfloat16)


def single_columns(width):
    return [max(LANES, width * single // (SINGLE_OF * LANES) * LANES) for single in SINGLE]


def tree_kernel(
    tokens, ids_hbm, values_hbm, wg_hbm, wu_hbm, wd_hbm, out_hbm,
    out, ids, values, tables, x, wg, wu, wd, pin, pout, own, rs_a, rs_b, yr_a, yr_b,
    out_sem, gate_sem, weight_sem, own_sem, za_send, za_recv, zb_send, zb_recv, ya_send, ya_recv, yb_send, yb_recv,
    yt_send, yt_recv, zt_send, zt_recv, pat_send, pat_recv,
    pa_send, pa_recv, pp_send, pp_recv, ra_send, ra_recv, rb_send, rb_recv,
    yra_send, yra_recv, yrb_send, yrb_recv,
):
    tok, width = tokens.shape
    wa = single_columns(width)
    rows = tok // SLICES
    node = lax.axis_index("node")
    other_core = {"local": 1 - lax.axis_index("local")}
    plane, column = node // COLUMNS, node % COLUMNS
    across = {"node": node + 1 - 2 * column}
    flip = jnp.where(plane >= PLANES // 2, 1, 0)
    near = plane * (1 - flip) + (PLANES - 1 - plane) * flip

    def actual(t):
        return t * (1 - flip) + (PLANES - 1 - t) * flip

    def along(s):
        return {"node": node + COLUMNS * s * (1 - 2 * flip)}

    def upward(s):
        return (1 - flip) if s > 0 else flip

    cols_b = [pl.ds(wa[h], width - wa[h]) for h in range(SLICES)]
    low_b = [pl.ds(0, width - wa[h]) for h in range(SLICES)]
    bounds = [[wa[h] // LANES * j // PIECES * LANES for j in range(PIECES + 1)] for h in range(SLICES)]
    cols_a = [
        [pl.ds(bounds[h][j], bounds[h][j + 1] - bounds[h][j]) for j in range(PIECES)]
        for h in range(SLICES)
    ]

    keeps = [
        pltpu.make_async_copy(
            tokens.at[pl.ds(h * rows, rows)],
            x.at[plane, h, pl.ds(0, rows)],
            own_sem.at[h],
        )
        for h in range(SLICES)
    ]
    gates = [
        pltpu.make_async_copy(src, dst, gate_sem.at[k])
        for k, (src, dst) in enumerate(((ids_hbm, ids), (values_hbm, values)))
    ]
    for keep in keeps + gates:
        keep.start()
    loads = [
        pltpu.make_async_copy(src, dst, weight_sem.at[k])
        for k, (src, dst) in enumerate(((wg_hbm, wg), (wu_hbm, wu), (wd_hbm, wd)))
    ]

    barrier = pltpu.get_barrier_semaphore()
    for target in (other_core, across, along(1)):
        pl.semaphore_signal(barrier, inc=1, device_id=target, device_id_type=MESH)

    @pl.when(near > 0)
    def _():
        pl.semaphore_signal(barrier, inc=1, device_id=along(-1), device_id_type=MESH)

    pl.semaphore_wait(barrier, 3 + jnp.where(near > 0, 1, 0))
    for keep in keeps:
        keep.wait()
    for load in loads:
        load.start()

    first, second = pl.ds(0, rows), pl.ds(rows, rows)
    part = (first, second)

    def copy(src, dst, send, recv, target):
        return pltpu.make_async_remote_copy(
            src_ref=src, dst_ref=dst, send_sem=send, recv_sem=recv,
            device_id=target, device_id_type=MESH,
        )

    def fill_table():
        for gate in gates:
            gate.wait()
        table_row = lax.broadcasted_iota(jnp.int32, (tables.shape[3], tok), 0)
        table = jnp.zeros(table_row.shape, jnp.float32)
        for choice in range(ids.shape[0]):
            chosen = table_row == ids[pl.ds(choice, 1), :]
            weight = values[pl.ds(choice, 1), :].astype(jnp.float32)
            table += jnp.where(chosen, weight, 0.0)
        tables[plane, 0, 0, :, pl.ds(0, tok)] = table.astype(jnp.bfloat16)

    def sums(t, s):
        up = upward(s)
        return up, actual(t) - up

    def send(op):
        kind, t, h = op[:3]
        p = actual(t)
        if kind == "zA":
            j, s = op[3:]
            ref = x.at[p, h, first, cols_a[h][j]]
            return copy(ref, ref, za_send.at[max(s, 0), p, h, j], za_recv.at[p, h, j], along(s))
        if kind == "zB":
            j, s = op[3:]
            ref = x.at[p, h, part[j], cols_b[h]]
            return copy(ref, ref, zb_send.at[max(s, 0), p, h, j], zb_recv.at[p, h, j], along(s))
        if kind == "yA":
            j = op[3]
            return copy(
                x.at[p, h, first, cols_a[h][j]], x.at[p, h, second, cols_a[h][j]],
                ya_send.at[p, h, j], ya_recv.at[p, h, j], across,
            )
        if kind == "yB":
            return copy(
                x.at[p, h, first, cols_b[h]], x.at[p, h, second, cols_b[h]],
                yb_send.at[h], yb_recv.at[h], across,
            )
        if kind == "yT":
            return copy(tables.at[p, 0, 0], tables.at[p, 0, 1], yt_send.at[0], yt_recv.at[0], across)
        if kind == "zT":
            s = op[3]
            ref = tables.at[p, 0]
            return copy(ref, ref, zt_send.at[max(s, 0), p], zt_recv.at[p], along(s))
        if kind == "paT":
            return copy(
                tables.at[p, 0], tables.at[p, 1], pat_send.at[p], pat_recv.at[p], other_core
            )
        if kind == "pa":
            return copy(
                x.at[p, h, part[op[3]]], x.at[p, h, pl.ds((2 + op[3]) * rows, rows)],
                pa_send.at[p, h, op[3]], pa_recv.at[p, h, op[3]], other_core,
            )
        if kind == "yr":
            j = op[3]
            return copy(
                pin.at[p, h, second, cols_a[h][j]], yr_a.at[p, h, :, cols_a[h][j]],
                yra_send.at[p, h, j], yra_recv.at[p, h, j], across,
            )
        if kind == "FB1":
            return copy(
                pin.at[p, h, second, cols_b[h]], yr_b.at[h, :, low_b[h]], yrb_send.at[h], yrb_recv.at[h], across
            )
        j, s = op[3:]
        up, place = sums(t, s)
        if kind == "TA":
            return copy(
                pin.at[p, h, first, cols_a[h][j]], rs_a.at[up, place, h, :, cols_a[h][j]],
                ra_send.at[p, h, j], ra_recv.at[up, p, h, j], along(s),
            )
        return copy(
            pin.at[p, h, part[j], cols_b[h]], rs_b.at[up, place, h, part[j], low_b[h]],
            rb_send.at[p, h, j], rb_recv.at[up, p, h, j], along(s),
        )

    def pp(p, h, slot):
        return copy(pout.at[slot], pin.at[p, h], pp_send.at[slot], pp_recv.at[p, h], other_core)

    def leave(h, j):
        at = (pl.ds(h * rows, rows), [*cols_a[h], cols_b[h]][j])
        return pltpu.make_async_copy(out.at[at], out_hbm.at[at], out_sem.at[h, j])

    def add_up(dst, terms, size):
        step = chunk_of(size, 3072)

        @pl.loop(0, size // step)
        def _(k):
            at = pl.multiple_of(k * step, LANES)
            total = terms[0](at, step).astype(jnp.float32)
            for term in terms[1:]:
                total += term(at, step).astype(jnp.float32)
            dst(at, step, total.astype(jnp.bfloat16))

    def run(op, z, slot_of):
        kind, t, h = op[:3]
        p = actual(t)
        towards = 1 if t > z else -1
        sides = [s for s in (1, -1) if 0 <= z + s < PLANES]
        if kind in ("zA", "zB", "zT", "yA", "yB", "yT", "pa", "paT", "yr"):
            send(op).start()
        elif kind == "wzT":
            send(("zT", t, h, 1)).wait_recv()
        elif kind == "wyT":
            send(("yT", t, h)).wait_recv()
        elif kind == "wpT":
            send(("paT", t, h)).wait_recv()
        elif kind == "wzA":
            send(("zA", t, h, op[3], 1)).wait_recv()
        elif kind == "wzB":
            send(("zB", t, h, op[3], 1)).wait_recv()
        elif kind == "wyA":
            send(("yA", *op[1:])).wait_recv()
        elif kind == "wyB":
            send(("yB", t, h)).wait_recv()
        elif kind == "S":
            slot = slot_of[(t, h)]
            pp(p, h, slot).wait_recv()

            def joined(at, step, value):
                pin[p, h, :, pl.ds(at, step)] = value

            add_up(
                joined,
                (
                    lambda at, step: own[slot, :, pl.ds(at, step)],
                    lambda at, step: pin[p, h, :, pl.ds(at, step)],
                ),
                width,
            )
        elif kind == "TB":
            j = op[3]
            if 0 <= z - towards < PLANES:
                up, place = sums(t, towards)
                send((*op, towards)).wait_recv()

                def passed(at, step, value):
                    pin[p, h, part[j], pl.ds(wa[h] + at, step)] = value

                add_up(
                    passed,
                    (
                        lambda at, step: pin[p, h, part[j], pl.ds(wa[h] + at, step)],
                        lambda at, step: rs_b[up, place, h, part[j], pl.ds(at, step)],
                    ),
                    width - wa[h],
                )
            send((*op, towards)).start()
        elif kind in ("TA", "FA"):
            j = op[3]
            send(("yr", *op[1:])).wait_recv()
            terms = [
                lambda at, step: pin[p, h, first, pl.ds(bounds[h][j] + at, step)],
                lambda at, step: yr_a[p, h, :, pl.ds(bounds[h][j] + at, step)],
            ]
            own_plane = kind == "FA"
            for s in [-s for s in sides] if own_plane else [towards]:
                if own_plane or 0 <= z - towards < PLANES:
                    up, place = sums(t, s)
                    send(("TA", t, h, j, s)).wait_recv()
                    terms.append(
                        lambda at, step, up=up, place=place: rs_a[
                            up, place, h, :, pl.ds(bounds[h][j] + at, step)
                        ]
                    )

            def finished(at, step, value):
                if own_plane:
                    out[pl.ds(h * rows, rows), pl.ds(bounds[h][j] + at, step)] = value
                else:
                    pin[p, h, first, pl.ds(bounds[h][j] + at, step)] = value

            add_up(finished, terms, bounds[h][j + 1] - bounds[h][j])
            if own_plane:
                leave(h, j).start()
            else:
                send((*op, towards)).start()
        elif kind in ("FB0", "FB1"):
            j = int(kind == "FB1")
            terms = [lambda at, step: pin[p, h, part[j], pl.ds(wa[h] + at, step)]]
            if j == 0:
                send(("FB1", t, h)).wait_recv()
                terms.append(lambda at, step: yr_b[h, :, pl.ds(at, step)])
            for s in sides:
                up, place = sums(t, -s)
                send(("TB", t, h, j, -s)).wait_recv()
                terms.append(
                    lambda at, step, up=up, place=place: rs_b[
                        up, place, h, part[j], pl.ds(at, step)
                    ]
                )

            def settled(at, step, value):
                if j == 0:
                    out[pl.ds(h * rows, rows), pl.ds(wa[h] + at, step)] = value
                else:
                    pin[p, h, second, pl.ds(wa[h] + at, step)] = value

            add_up(settled, terms, width - wa[h])
            if j == 1:
                send(op).start()
            else:
                leave(h, PIECES).start()

    def compute(k, p, h):
        slot = k % 2
        for side in range(2):
            copy(
                x.at[p, h, pl.ds(side * rows, rows)], x.at[p, h, pl.ds((2 + side) * rows, rows)],
                pa_send.at[p, h, side], pa_recv.at[p, h, side], other_core,
            ).wait_recv()

        @pl.when(k == 0)
        def _():
            loads[0].wait()
            loads[1].wait()

        @pl.when(k >= 2)
        def _():
            pp(p, h, slot).wait_send()

        gate = jnp.dot(x[p, h], wg[...], preferred_element_type=jnp.float32)
        up = jnp.dot(x[p, h], wu[...], preferred_element_type=jnp.float32)
        hidden = (gate / (1.0 + jnp.exp(-gate)) * up).astype(jnp.bfloat16)
        expert = lax.broadcasted_iota(jnp.int32, tables.shape[3:], 0) == node
        token = lax.broadcasted_iota(jnp.int32, (rows, LANES), 1) == (
            lax.broadcasted_iota(jnp.int32, (rows, LANES), 0) + h * rows
        )
        weights = []
        for core in range(2):
            for side in range(COLUMNS):
                table = tables[p, core, side].astype(jnp.float32)
                row = jnp.sum(jnp.where(expert, table, 0.0), axis=0, keepdims=True)
                weights.append(jnp.sum(jnp.where(token, row, 0.0), axis=1, keepdims=True))
        scale = jnp.concatenate(weights, axis=0)

        @pl.when(k == 0)
        def _():
            loads[2].wait()

        step = chunk_of(width, 1792)
        for c in range(width // step):
            cols = pl.ds(c * step, step)
            value = jnp.dot(hidden, wd[:, cols], preferred_element_type=jnp.float32) * scale
            own[slot, :, cols] = value[:2 * rows]
            pout[slot, :, cols] = value[2 * rows:].astype(jnp.bfloat16)
        pp(p, h, slot).start()

    items = [[group[-1][1:3] for group in groups[:-1]] for groups in SCHEDULE]
    count = len(items[0])

    @pl.loop(0, count)
    def _(k):
        for z, groups in enumerate(SCHEDULE):
            slot_of = {item: i % 2 for i, item in enumerate(items[z])}
            tabled = [
                op for op in groups[0]
                if op[0] == "yT"
            ]
            for i, group in enumerate(groups[:-1]):

                @pl.when((near == z) & (k == i))
                def _(group=group, z=z, slot_of=slot_of, at=tabled[0] if i == 0 else None):
                    for op in group[:-1]:
                        if op == at:
                            fill_table()
                        run(op, z, slot_of)

        t, h = 0, 0
        for z, of in enumerate(items):
            for i, item in enumerate(of):
                here = jnp.where(near == z, 1, 0) * jnp.where(k == i, 1, 0)
                t, h = t + here * item[0], h + here * item[1]
        compute(k, actual(t), h)

    for z, groups in enumerate(SCHEDULE):
        slot_of = {item: i % 2 for i, item in enumerate(items[z])}

        @pl.when(near == z)
        def _(groups=groups, z=z, slot_of=slot_of):
            for op in groups[-1]:
                run(op, z, slot_of)
            for group in groups:
                for op in group:
                    if op[0] in ("zA", "zB", "zT", "yA", "yB", "yT", "pa", "paT", "yr", "FB1"):
                        send(op).wait_send()
                    elif op[0] in ("TA", "TB"):
                        send((*op, 1 if op[1] > z else -1)).wait_send()
            for h in range(SLICES):
                for j in range(PIECES + 1):
                    leave(h, j).wait()
            for t, h in items[z][-2:]:
                pp(actual(t), h, slot_of[(t, h)]).wait_send()


def buffers(tok, width, hid, topk):
    wa = single_columns(width)
    rows = tok // SLICES
    kind = jnp.bfloat16
    return [
        pltpu.VMEM((tok, width), kind),
        pltpu.VMEM((topk, tok), jnp.int32),
        pltpu.VMEM((topk, tok), kind),
        pltpu.VMEM((PLANES, 2, COLUMNS, 16, LANES), kind),
        pltpu.VMEM((PLANES, SLICES, 4 * rows, width), kind),
        pltpu.VMEM((width, hid), kind),
        pltpu.VMEM((width, hid), kind),
        pltpu.VMEM((hid, width), kind),
        pltpu.VMEM((PLANES, SLICES, 2 * rows, width), kind),
        pltpu.VMEM((2, 2 * rows, width), kind),
        pltpu.VMEM((2, 2 * rows, width), jnp.float32),
        pltpu.VMEM((2, PLANES - 1, SLICES, rows, max(wa)), kind),
        pltpu.VMEM((2, PLANES - 1, SLICES, 2 * rows, width - min(wa)), kind),
        pltpu.VMEM((PLANES, SLICES, rows, max(wa)), kind),
        pltpu.VMEM((SLICES, rows, width - min(wa)), kind),
    ]


def by_trees(tokens, gate_ids, gate_values, w_gate, w_up, w_down):
    tok, width = tokens.shape
    anywhere = pl.BlockSpec(memory_space=pl.ANY)

    def dma(*shape):
        return pltpu.SemaphoreType.DMA(shape)

    each = (PLANES, SLICES)
    return pl.pallas_call(
        tree_kernel,
        out_shape=jax.ShapeDtypeStruct((tok, width), jnp.bfloat16),
        in_specs=[anywhere] * 6,
        out_specs=anywhere,
        scratch_shapes=[
            *buffers(tok, width, w_gate.shape[2], gate_ids.shape[1]),
            dma(SLICES, PIECES + 1), dma(2), dma(3), dma(SLICES),
            dma(2, *each, PIECES), dma(*each, PIECES), dma(2, *each, 2), dma(*each, 2),
            dma(*each, PIECES), dma(*each, PIECES), dma(SLICES), dma(SLICES),
            dma(1), dma(1), dma(2, PLANES), dma(PLANES), dma(PLANES), dma(PLANES),
            dma(*each, 2), dma(*each, 2), dma(2), dma(*each),
            dma(*each, PIECES), dma(2, *each, PIECES), dma(*each, 2), dma(2, *each, 2),
            dma(*each, PIECES), dma(*each, PIECES), dma(SLICES), dma(SLICES),
        ],
        compiler_params=pltpu.CompilerParams(
            collective_id=0, has_side_effects=True, vmem_limit_bytes=VMEM_LIMIT
        ),
    )(tokens, gate_ids.T, gate_values.T, w_gate[0], w_up[0], w_down[0])


def by_collectives(tokens, gate_ids, gate_values, w_gate, w_up, w_down):
    n = lax.axis_size("node")
    every = ("node", "local")
    weights = lax.all_gather(expert_weights(gate_ids, gate_values, n), every, axis=0, tiled=True)
    rows = lax.all_gather(tokens, every, axis=0, tiled=True)
    mine = (jnp.arange(n, dtype=jnp.int32) == lax.axis_index("node"))[None, :]
    scale = jnp.sum(jnp.where(mine, weights.astype(jnp.float32), 0.0), axis=1, keepdims=True)
    gate_act = jnp.dot(rows, w_gate[0], preferred_element_type=jnp.float32)
    up_act = jnp.dot(rows, w_up[0], preferred_element_type=jnp.float32)
    hidden = (jax.nn.silu(gate_act) * up_act).astype(jnp.bfloat16)
    partial_value = jnp.dot(hidden, w_down[0], preferred_element_type=jnp.float32) * scale
    return lax.psum_scatter(
        partial_value.astype(jnp.bfloat16), every, scatter_dimension=0, tiled=True
    )


def trees_fit(n, tok, width, hid, topk):
    if n != PLANES * COLUMNS or lax.axis_size("local") != 2 or tok % (16 * SLICES) or width % LANES:
        return False
    if width < 2 * LANES or tok > LANES or n > 16:
        return False
    size = 2**21
    for ref in buffers(tok, width, hid, topk):
        size += ref.inner_aval.size * ref.inner_aval.dtype.itemsize
    return size < VMEM_LIMIT


def per_device(tokens, gate_ids, gate_values, w_gate, w_up, w_down):
    n = lax.axis_size("node")
    args = (tokens, gate_ids, gate_values, w_gate, w_up, w_down)
    if trees_fit(n, *tokens.shape, w_gate.shape[2], gate_ids.shape[1]):
        return by_trees(*args)
    return by_collectives(*args)


def solution(mesh):
    return jax.shard_map(
        per_device,
        mesh=mesh,
        in_specs=(
            P(("rep", "node", "local"), None),
            P(("rep", "node", "local"), None),
            P(("rep", "node", "local"), None),
            P("node", None, "local"),
            P("node", None, "local"),
            P("node", "local", None),
        ),
        out_specs=P(("rep", "node", "local"), None),
        check_vma=False,
    )
```

```python
import functools

import jax
import jax.numpy as jnp
from jax import lax
from jax.experimental import pallas as pl
from jax.experimental.pallas import tpu as pltpu
from jax.sharding import PartitionSpec as P

MESH = pl.DeviceIdType.MESH
LANES = 128
VMEM_LIMIT = 67_000_000
PLANES = 4
COLUMNS = 2
SLICES = 2
SINGLE = (34, 33)
SINGLE_OF = 56
PIECES = 2

(ZA, ZB, ZT, YA, YB, YT, PA, PAT, WZA, WZB, WZT, WYA,
 WYB, WYT, WPT, WORK, JOIN, YR, TA, TB, FA, FB0, FB1) = range(23)

SCHEDULE = (
    (
        ((ZA, 0, 0, 1, 1), (YB, 0, 0), (ZA, 0, 1, 1, 1), (YA, 0, 0, 1), (WZA, 1, 1, 1), (ZA, 0, 1, 0, 1), (YT, 0, 0), (ZA, 0, 0, 0, 1), (YA, 1, 1, 1), (WZA, 1, 1, 0), (ZB, 0, 0, 0, 1), (WYB, 0, 0), (YA, 0, 0, 0), (YA, 1, 1, 0), (WYA, 1, 1, 1), (WYT, 0, 0), (YB, 0, 1), (ZT, 0, 0, 1), (ZB, 0, 0, 1, 1), (YA, 0, 1, 0), (WZT, 1, 0), (ZB, 0, 1, 0, 1), (WZB, 1, 1, 0), (PA, 1, 1, 0), (WZB, 1, 1, 1), (WYA, 1, 1, 0), (PAT, 1, 0), (WZT, 2, 0), (PA, 1, 1, 1), (WPT, 1, 0), (WZA, 2, 1, 0), (YA, 2, 1, 0), (WORK, 1, 1),),
        ((WYB, 0, 1), (WZA, 2, 1, 1), (ZB, 0, 1, 1, 1), (YA, 2, 1, 1), (JOIN, 1, 1), (YR, 1, 1, 0), (PAT, 2, 0), (TB, 1, 1, 0), (WZB, 2, 1, 0), (TB, 1, 1, 1), (WYA, 2, 1, 0), (PA, 2, 1, 0), (WZB, 2, 1, 1), (YR, 1, 1, 1), (WYA, 2, 1, 1), (PA, 2, 1, 1), (WPT, 2, 0), (WYA, 0, 0, 1), (WZA, 3, 0, 0), (PAT, 0, 0), (YA, 3, 0, 0), (TA, 1, 1, 0), (WORK, 2, 1),),
        ((WYA, 0, 0, 0), (WZA, 3, 0, 1), (YA, 3, 0, 1), (TA, 1, 1, 1), (JOIN, 2, 1), (YR, 2, 1, 1), (TB, 2, 1, 0), (PA, 0, 0, 1), (YR, 2, 1, 0), (YA, 0, 1, 1), (WZT, 3, 0), (WZB, 3, 0, 0), (PAT, 3, 0), (WPT, 3, 0), (WZB, 3, 0, 1), (WYA, 3, 0, 0), (PA, 3, 0, 0), (WYA, 3, 0, 1), (TB, 2, 1, 1), (PA, 0, 0, 0), (PA, 3, 0, 1), (TA, 2, 1, 1), (WZA, 3, 1, 1), (YA, 3, 1, 1), (WORK, 3, 0),),
        ((WPT, 0, 0), (WZA, 3, 1, 0), (YA, 3, 1, 0), (WYA, 0, 1, 1), (TA, 2, 1, 0), (JOIN, 3, 0), (TB, 3, 0, 1), (PA, 0, 1, 0), (YR, 3, 0, 1), (WZB, 3, 1, 0), (PA, 3, 1, 0), (YR, 3, 0, 0), (WORK, 0, 0),),
        ((WYA, 3, 1, 0), (WYA, 3, 1, 1), (WZB, 3, 1, 1), (TB, 3, 0, 0), (PA, 3, 1, 1), (WZA, 2, 0, 0), (YA, 2, 0, 0), (JOIN, 0, 0), (TA, 3, 0, 1), (YR, 0, 0, 1), (WORK, 3, 1),),
        ((WZA, 2, 0, 1), (YA, 2, 0, 1), (WYA, 0, 1, 0), (TA, 3, 0, 0), (JOIN, 3, 1), (WZB, 2, 0, 0), (TB, 3, 1, 1), (YR, 3, 1, 1), (WYA, 2, 0, 0), (WZB, 2, 0, 1), (WYA, 2, 0, 1), (PA, 2, 0, 1), (YR, 3, 1, 0), (PA, 2, 0, 0), (TB, 3, 1, 0), (WZA, 1, 0, 0), (YA, 1, 0, 0), (TA, 3, 1, 1), (WORK, 2, 0),),
        ((PA, 0, 1, 1), (WZA, 1, 0, 1), (YA, 1, 0, 1), (TA, 3, 1, 0), (JOIN, 2, 0), (YR, 2, 0, 1), (YR, 0, 0, 0), (TB, 2, 0, 1), (TB, 2, 0, 0), (WZB, 1, 0, 0), (PA, 1, 0, 0), (WORK, 0, 1),),
        ((WYA, 1, 0, 0), (WYA, 1, 0, 1), (WZB, 1, 0, 1), (PA, 1, 0, 1), (YR, 2, 0, 0), (JOIN, 0, 1), (TA, 2, 0, 1), (YR, 0, 1, 0), (WORK, 1, 0),),
        ((TA, 2, 0, 0), (YR, 0, 1, 1), (JOIN, 1, 0), (TB, 1, 0, 1), (TB, 1, 0, 0), (YR, 1, 0, 1), (YR, 1, 0, 0), (FB1, 0, 0), (FB1, 0, 1), (FA, 0, 1, 1), (TA, 1, 0, 1), (FA, 0, 0, 0), (FA, 0, 0, 1), (TA, 1, 0, 0), (FB0, 0, 0), (FA, 0, 1, 0), (FB0, 0, 1),),
    ),
    (
        ((ZA, 1, 1, 1, -1), (ZA, 1, 1, 0, -1), (ZA, 1, 1, 1, 1), (YT, 1, 0), (YB, 1, 1), (ZB, 1, 1, 0, 1), (YA, 1, 1, 1), (ZB, 1, 1, 0, -1), (WYB, 1, 1), (ZA, 1, 1, 0, 1), (WYT, 1, 0), (WZA, 2, 1, 1), (YB, 1, 0), (YA, 1, 1, 0), (ZT, 1, 0, 1), (WZA, 0, 0, 1), (ZB, 1, 1, 1, 1), (ZT, 1, 0, -1), (ZB, 1, 1, 1, -1), (WZA, 2, 1, 0), (WZT, 2, 0), (WZA, 0, 0, 0), (ZT, 2, 0, -1), (YA, 0, 0, 1), (ZA, 0, 0, 0, 1), (ZA, 2, 1, 0, -1), (PAT, 1, 0), (WYA, 1, 1, 0), (PA, 1, 0, 0), (WZB, 2, 1, 1), (ZA, 2, 1, 1, -1), (WZA, 0, 1, 1), (YA, 2, 1, 0), (ZA, 0, 0, 1, 1), (WZT, 0, 0), (WYA, 1, 1, 1), (ZT, 0, 0, 1), (PA, 1, 1, 1), (YA, 0, 0, 0), (WZB, 2, 1, 0), (WZA, 3, 0, 0), (YA, 2, 1, 1), (ZA, 0, 1, 1, 1), (ZB, 2, 1, 1, -1), (ZB, 2, 1, 0, -1), (WPT, 1, 0), (PAT, 0, 0), (WZT, 3, 0), (WZB, 0, 0, 0), (WZA, 3, 0, 1), (WZB, 0, 0, 1), (WZA, 0, 1, 0), (YA, 0, 1, 1), (ZB, 0, 0, 0, 1), (ZA, 3, 0, 0, -1), (ZA, 3, 0, 1, -1), (PA, 1, 1, 0), (ZT, 3, 0, -1), (PAT, 2, 0), (WPT, 0, 0), (YA, 3, 0, 1), (ZB, 0, 0, 1, 1), (WORK, 1, 1),),
        ((PA, 2, 1, 0), (WZA, 3, 1, 1), (ZA, 0, 1, 0, 1), (WYA, 2, 1, 1), (WZB, 0, 1, 0), (ZB, 0, 1, 0, 1), (WYA, 2, 1, 0), (WYA, 0, 0, 0), (WYA, 0, 1, 1), (PA, 0, 1, 0), (PA, 2, 1, 1), (YA, 0, 1, 0), (WPT, 2, 0), (ZA, 1, 0, 0, 1), (YA, 1, 0, 0), (JOIN, 1, 1), (WZB, 3, 0, 1), (YA, 3, 0, 0), (WZB, 3, 0, 0), (WZB, 0, 1, 1), (ZB, 3, 0, 0, -1), (ZB, 3, 0, 1, -1), (PAT, 3, 0), (PA, 0, 0, 0), (WORK, 2, 1),),
        ((WZA, 3, 1, 0), (YA, 1, 0, 1), (ZB, 0, 1, 1, 1), (WYA, 0, 1, 0), (WZB, 3, 1, 0), (WPT, 3, 0), (WYB, 1, 0), (ZA, 3, 1, 1, -1), (YA, 3, 1, 0), (PA, 3, 1, 0), (PA, 3, 0, 0), (WYA, 3, 0, 0), (YR, 1, 1, 1), (WYA, 3, 0, 1), (PA, 3, 0, 1), (WZA, 2, 0, 0), (WYA, 0, 0, 1), (PA, 0, 0, 1), (ZA, 3, 1, 0, -1), (ZB, 1, 0, 0, 1), (JOIN, 2, 1), (YA, 2, 0, 0), (ZA, 1, 0, 1, 1), (YA, 3, 1, 1), (WZB, 3, 1, 1), (ZB, 3, 1, 0, -1), (PA, 0, 1, 1), (WORK, 3, 0),),
        ((ZB, 3, 1, 1, -1), (YR, 2, 1, 1), (ZA, 2, 0, 0, -1), (WYA, 3, 1, 0), (ZB, 1, 0, 1, 1), (WORK, 0, 0),),
        ((WZB, 2, 0, 0), (TB, 2, 1, 1), (WYA, 2, 0, 0), (WZA, 2, 0, 1), (YR, 2, 1, 0), (JOIN, 3, 0), (WYA, 1, 0, 1), (WYA, 3, 1, 1), (ZA, 2, 0, 1, -1), (YA, 2, 0, 1), (YR, 1, 1, 0), (WZB, 2, 0, 1), (ZB, 2, 0, 0, -1), (TB, 2, 1, 0), (WORK, 0, 1),),
        ((TA, 2, 1, 0), (WYA, 1, 0, 0), (PA, 3, 1, 1), (JOIN, 0, 0), (ZB, 2, 0, 1, -1), (YR, 3, 0, 1), (PA, 2, 0, 0), (ZA, 1, 0, 0, -1), (TB, 3, 0, 0), (JOIN, 0, 1), (PA, 1, 0, 1), (WORK, 3, 1),),
        ((ZA, 1, 0, 1, -1), (YR, 3, 0, 0), (ZB, 1, 0, 0, -1), (YR, 0, 0, 1), (FA, 1, 1, 0), (WYA, 2, 0, 1), (TB, 3, 0, 1), (JOIN, 3, 1), (YR, 3, 1, 1), (FB1, 1, 1), (YR, 0, 1, 0), (PA, 2, 0, 1), (YR, 0, 1, 1), (TA, 3, 0, 1), (TB, 3, 1, 1), (ZB, 1, 0, 1, -1), (WORK, 2, 0),),
        ((YR, 3, 1, 0), (TB, 0, 0, 1), (TA, 3, 0, 0), (TA, 0, 0, 1), (YR, 0, 0, 0), (TA, 3, 1, 1), (TB, 0, 0, 0), (TA, 2, 1, 1), (TB, 3, 1, 0), (JOIN, 2, 0), (YR, 2, 0, 1), (WORK, 1, 0),),
        ((TA, 0, 1, 1), (JOIN, 1, 0), (TA, 3, 1, 0), (TB, 2, 0, 1), (FB0, 1, 1), (TB, 2, 0, 0), (YR, 2, 0, 0), (TB, 0, 1, 1), (TA, 0, 0, 0), (TA, 0, 1, 0), (YR, 1, 0, 0), (YR, 1, 0, 1), (TA, 2, 0, 1), (TA, 2, 0, 0), (FB1, 1, 0), (TB, 0, 1, 0), (FA, 1, 0, 1), (FB0, 1, 0), (FA, 1, 1, 1), (FA, 1, 0, 0),),
    ),
)


def chunk_of(size, most=1024):
    chunk = most
    while size % chunk:
        chunk -= LANES
    return chunk


def expert_weights(gate_ids, gate_values, columns):
    expert_row = jnp.arange(columns, dtype=jnp.int32)
    return jnp.sum(
        jnp.where(
            gate_ids[:, :, None] == expert_row[None, None, :],
            gate_values.astype(jnp.float32)[:, :, None],
            jnp.float32(0.0),
        ),
        axis=1,
    ).astype(jnp.bfloat16)


def single_columns(width):
    return [max(LANES, width * single // (SINGLE_OF * LANES) * LANES) for single in SINGLE]


def tree_kernel(
    tokens, ids_hbm, values_hbm, wg_hbm, wu_hbm, wd_hbm, out_hbm,
    out, ids, values, tables, x, wg, wu, wd, pin, pout, own, rs_a, rs_b, yr_a, yr_b,
    out_sem, gate_sem, weight_sem, own_sem, za_send, za_recv, zb_send, zb_recv, ya_send, ya_recv, yb_send, yb_recv,
    yt_send, yt_recv, zt_send, zt_recv, pat_send, pat_recv,
    pa_send, pa_recv, pp_send, pp_recv, ra_send, ra_recv, rb_send, rb_recv,
    yra_send, yra_recv, yrb_send, yrb_recv,
):
    tok, width = tokens.shape
    wa = single_columns(width)
    rows = tok // SLICES
    node = lax.axis_index("node")
    other_core = {"local": 1 - lax.axis_index("local")}
    plane, column = node // COLUMNS, node % COLUMNS
    across = {"node": node + 1 - 2 * column}
    flip = jnp.where(plane >= PLANES // 2, 1, 0)
    near = plane * (1 - flip) + (PLANES - 1 - plane) * flip

    def actual(t):
        return t * (1 - flip) + (PLANES - 1 - t) * flip

    def along(s):
        return {"node": node + COLUMNS * s * (1 - 2 * flip)}

    def upward(s):
        return (1 - flip) if s > 0 else flip

    cols_b = [pl.ds(wa[h], width - wa[h]) for h in range(SLICES)]
    low_b = [pl.ds(0, width - wa[h]) for h in range(SLICES)]
    bounds = [[wa[h] // LANES * j // PIECES * LANES for j in range(PIECES + 1)] for h in range(SLICES)]
    cols_a = [
        [pl.ds(bounds[h][j], bounds[h][j + 1] - bounds[h][j]) for j in range(PIECES)]
        for h in range(SLICES)
    ]

    keeps = [
        pltpu.make_async_copy(
            tokens.at[pl.ds(h * rows, rows)],
            x.at[plane, h, pl.ds(0, rows)],
            own_sem.at[h],
        )
        for h in range(SLICES)
    ]
    gates = [
        pltpu.make_async_copy(src, dst, gate_sem.at[k])
        for k, (src, dst) in enumerate(((ids_hbm, ids), (values_hbm, values)))
    ]
    for keep in keeps + gates:
        keep.start()
    loads = [
        pltpu.make_async_copy(src, dst, weight_sem.at[k])
        for k, (src, dst) in enumerate(((wg_hbm, wg), (wu_hbm, wu), (wd_hbm, wd)))
    ]

    barrier = pltpu.get_barrier_semaphore()
    for target in (other_core, across, along(1)):
        pl.semaphore_signal(barrier, inc=1, device_id=target, device_id_type=MESH)

    @pl.when(near > 0)
    def _():
        pl.semaphore_signal(barrier, inc=1, device_id=along(-1), device_id_type=MESH)

    pl.semaphore_wait(barrier, 3 + jnp.where(near > 0, 1, 0))
    for keep in keeps:
        keep.wait()
    for load in loads:
        load.start()

    first, second = pl.ds(0, rows), pl.ds(rows, rows)
    part = (first, second)

    def copy(src, dst, send, recv, target):
        return pltpu.make_async_remote_copy(
            src_ref=src, dst_ref=dst, send_sem=send, recv_sem=recv,
            device_id=target, device_id_type=MESH,
        )

    def fill_table():
        for gate in gates:
            gate.wait()
        table_row = lax.broadcasted_iota(jnp.int32, (tables.shape[3], tok), 0)
        table = jnp.zeros(table_row.shape, jnp.float32)
        for choice in range(ids.shape[0]):
            chosen = table_row == ids[pl.ds(choice, 1), :]
            weight = values[pl.ds(choice, 1), :].astype(jnp.float32)
            table += jnp.where(chosen, weight, 0.0)
        tables[plane, 0, 0, :, pl.ds(0, tok)] = table.astype(jnp.bfloat16)

    def sums(t, s):
        up = upward(s)
        return up, actual(t) - up

    def send(op):
        kind, t, h = op[:3]
        p = actual(t)
        if kind == ZA:
            j, s = op[3:]
            ref = x.at[p, h, first, cols_a[h][j]]
            return copy(ref, ref, za_send.at[max(s, 0), p, h, j], za_recv.at[p, h, j], along(s))
        if kind == ZB:
            j, s = op[3:]
            ref = x.at[p, h, part[j], cols_b[h]]
            return copy(ref, ref, zb_send.at[max(s, 0), p, h, j], zb_recv.at[p, h, j], along(s))
        if kind == YA:
            j = op[3]
            return copy(
                x.at[p, h, first, cols_a[h][j]], x.at[p, h, second, cols_a[h][j]],
                ya_send.at[p, h, j], ya_recv.at[p, h, j], across,
            )
        if kind == YB:
            return copy(
                x.at[p, h, first, cols_b[h]], x.at[p, h, second, cols_b[h]],
                yb_send.at[h], yb_recv.at[h], across,
            )
        if kind == YT:
            return copy(tables.at[p, 0, 0], tables.at[p, 0, 1], yt_send.at[0], yt_recv.at[0], across)
        if kind == ZT:
            s = op[3]
            ref = tables.at[p, 0]
            return copy(ref, ref, zt_send.at[max(s, 0), p], zt_recv.at[p], along(s))
        if kind == PAT:
            return copy(
                tables.at[p, 0], tables.at[p, 1], pat_send.at[p], pat_recv.at[p], other_core
            )
        if kind == PA:
            return copy(
                x.at[p, h, part[op[3]]], x.at[p, h, pl.ds((2 + op[3]) * rows, rows)],
                pa_send.at[p, h, op[3]], pa_recv.at[p, h, op[3]], other_core,
            )
        if kind == YR:
            j = op[3]
            return copy(
                pin.at[p, h, second, cols_a[h][j]], yr_a.at[p, h, :, cols_a[h][j]],
                yra_send.at[p, h, j], yra_recv.at[p, h, j], across,
            )
        if kind == FB1:
            return copy(
                pin.at[p, h, second, cols_b[h]], yr_b.at[h, :, low_b[h]], yrb_send.at[h], yrb_recv.at[h], across
            )
        j, s = op[3:]
        up, place = sums(t, s)
        if kind == TA:
            return copy(
                pin.at[p, h, first, cols_a[h][j]], rs_a.at[up, place, h, :, cols_a[h][j]],
                ra_send.at[p, h, j], ra_recv.at[up, p, h, j], along(s),
            )
        return copy(
            pin.at[p, h, part[j], cols_b[h]], rs_b.at[up, place, h, part[j], low_b[h]],
            rb_send.at[p, h, j], rb_recv.at[up, p, h, j], along(s),
        )

    def pp(p, h, slot):
        return copy(pout.at[slot], pin.at[p, h], pp_send.at[slot], pp_recv.at[p, h], other_core)

    def leave(h, j):
        at = (pl.ds(h * rows, rows), [*cols_a[h], cols_b[h]][j])
        return pltpu.make_async_copy(out.at[at], out_hbm.at[at], out_sem.at[h, j])

    def add_up(dst, terms, size):
        step = chunk_of(size, 3072)

        @pl.loop(0, size // step)
        def _(k):
            at = pl.multiple_of(k * step, LANES)
            total = terms[0](at, step).astype(jnp.float32)
            for term in terms[1:]:
                total += term(at, step).astype(jnp.float32)
            dst(at, step, total.astype(jnp.bfloat16))

    def run(op, z, slot_of):
        kind, t, h = op[:3]
        p = actual(t)
        towards = 1 if t > z else -1
        sides = [s for s in (1, -1) if 0 <= z + s < PLANES]
        if kind in (ZA, ZB, ZT, YA, YB, YT, PA, PAT, YR):
            send(op).start()
        elif kind == WZT:
            send((ZT, t, h, 1)).wait_recv()
        elif kind == WYT:
            send((YT, t, h)).wait_recv()
        elif kind == WPT:
            send((PAT, t, h)).wait_recv()
        elif kind == WZA:
            send((ZA, t, h, op[3], 1)).wait_recv()
        elif kind == WZB:
            send((ZB, t, h, op[3], 1)).wait_recv()
        elif kind == WYA:
            send((YA, *op[1:])).wait_recv()
        elif kind == WYB:
            send((YB, t, h)).wait_recv()
        elif kind == JOIN:
            slot = slot_of[(t, h)]
            pp(p, h, slot).wait_recv()

            def joined(at, step, value):
                pin[p, h, :, pl.ds(at, step)] = value

            add_up(
                joined,
                (
                    lambda at, step: own[slot, :, pl.ds(at, step)],
                    lambda at, step: pin[p, h, :, pl.ds(at, step)],
                ),
                width,
            )
        elif kind == TB:
            j = op[3]
            if 0 <= z - towards < PLANES:
                up, place = sums(t, towards)
                send((*op, towards)).wait_recv()

                def passed(at, step, value):
                    pin[p, h, part[j], pl.ds(wa[h] + at, step)] = value

                add_up(
                    passed,
                    (
                        lambda at, step: pin[p, h, part[j], pl.ds(wa[h] + at, step)],
                        lambda at, step: rs_b[up, place, h, part[j], pl.ds(at, step)],
                    ),
                    width - wa[h],
                )
            send((*op, towards)).start()
        elif kind in (TA, FA):
            j = op[3]
            send((YR, *op[1:])).wait_recv()
            terms = [
                lambda at, step: pin[p, h, first, pl.ds(bounds[h][j] + at, step)],
                lambda at, step: yr_a[p, h, :, pl.ds(bounds[h][j] + at, step)],
            ]
            own_plane = kind == FA
            for s in [-s for s in sides] if own_plane else [towards]:
                if own_plane or 0 <= z - towards < PLANES:
                    up, place = sums(t, s)
                    send((TA, t, h, j, s)).wait_recv()
                    terms.append(
                        lambda at, step, up=up, place=place: rs_a[
                            up, place, h, :, pl.ds(bounds[h][j] + at, step)
                        ]
                    )

            def finished(at, step, value):
                if own_plane:
                    out[pl.ds(h * rows, rows), pl.ds(bounds[h][j] + at, step)] = value
                else:
                    pin[p, h, first, pl.ds(bounds[h][j] + at, step)] = value

            add_up(finished, terms, bounds[h][j + 1] - bounds[h][j])
            if own_plane:
                leave(h, j).start()
            else:
                send((*op, towards)).start()
        elif kind in (FB0, FB1):
            j = int(kind == FB1)
            terms = [lambda at, step: pin[p, h, part[j], pl.ds(wa[h] + at, step)]]
            if j == 0:
                send((FB1, t, h)).wait_recv()
                terms.append(lambda at, step: yr_b[h, :, pl.ds(at, step)])
            for s in sides:
                up, place = sums(t, -s)
                send((TB, t, h, j, -s)).wait_recv()
                terms.append(
                    lambda at, step, up=up, place=place: rs_b[
                        up, place, h, part[j], pl.ds(at, step)
                    ]
                )

            def settled(at, step, value):
                if j == 0:
                    out[pl.ds(h * rows, rows), pl.ds(wa[h] + at, step)] = value
                else:
                    pin[p, h, second, pl.ds(wa[h] + at, step)] = value

            add_up(settled, terms, width - wa[h])
            if j == 1:
                send(op).start()
            else:
                leave(h, PIECES).start()

    def compute(k, p, h):
        slot = k % 2
        for side in range(2):
            copy(
                x.at[p, h, pl.ds(side * rows, rows)], x.at[p, h, pl.ds((2 + side) * rows, rows)],
                pa_send.at[p, h, side], pa_recv.at[p, h, side], other_core,
            ).wait_recv()

        @pl.when(k == 0)
        def _():
            loads[0].wait()
            loads[1].wait()

        @pl.when(k >= 2)
        def _():
            pp(p, h, slot).wait_send()

        gate = jnp.dot(x[p, h], wg[...], preferred_element_type=jnp.float32)
        up = jnp.dot(x[p, h], wu[...], preferred_element_type=jnp.float32)
        hidden = (gate / (1.0 + jnp.exp(-gate)) * up).astype(jnp.bfloat16)
        expert = lax.broadcasted_iota(jnp.int32, tables.shape[3:], 0) == node
        token = lax.broadcasted_iota(jnp.int32, (rows, LANES), 1) == (
            lax.broadcasted_iota(jnp.int32, (rows, LANES), 0) + h * rows
        )
        weights = []
        for core in range(2):
            for side in range(COLUMNS):
                table = tables[p, core, side].astype(jnp.float32)
                row = jnp.sum(jnp.where(expert, table, 0.0), axis=0, keepdims=True)
                weights.append(jnp.sum(jnp.where(token, row, 0.0), axis=1, keepdims=True))
        scale = jnp.concatenate(weights, axis=0)

        @pl.when(k == 0)
        def _():
            loads[2].wait()

        step = chunk_of(width, 1792)
        for c in range(width // step):
            cols = pl.ds(c * step, step)
            value = jnp.dot(hidden, wd[:, cols], preferred_element_type=jnp.float32) * scale
            own[slot, :, cols] = value[:2 * rows]
            pout[slot, :, cols] = value[2 * rows:].astype(jnp.bfloat16)
        pp(p, h, slot).start()

    items = [[group[-1][1:3] for group in groups[:-1]] for groups in SCHEDULE]
    count = len(items[0])

    @pl.loop(0, count)
    def _(k):
        for z, groups in enumerate(SCHEDULE):
            slot_of = {item: i % 2 for i, item in enumerate(items[z])}
            tabled = [
                op for op in groups[0]
                if op[0] == YT
            ]
            for i, group in enumerate(groups[:-1]):

                @pl.when((near == z) & (k == i))
                def _(group=group, z=z, slot_of=slot_of, at=tabled[0] if i == 0 else None):
                    for op in group[:-1]:
                        if op == at:
                            fill_table()
                        run(op, z, slot_of)

        t, h = 0, 0
        for z, of in enumerate(items):
            for i, item in enumerate(of):
                here = jnp.where(near == z, 1, 0) * jnp.where(k == i, 1, 0)
                t, h = t + here * item[0], h + here * item[1]
        compute(k, actual(t), h)

    for z, groups in enumerate(SCHEDULE):
        slot_of = {item: i % 2 for i, item in enumerate(items[z])}

        @pl.when(near == z)
        def _(groups=groups, z=z, slot_of=slot_of):
            for op in groups[-1]:
                run(op, z, slot_of)
            for group in groups:
                for op in group:
                    if op[0] in (ZA, ZB, ZT, YA, YB, YT, PA, PAT, YR, FB1):
                        send(op).wait_send()
                    elif op[0] in (TA, TB):
                        send((*op, 1 if op[1] > z else -1)).wait_send()
            for h in range(SLICES):
                for j in range(PIECES + 1):
                    leave(h, j).wait()
            for t, h in items[z][-2:]:
                pp(actual(t), h, slot_of[(t, h)]).wait_send()


def buffers(tok, width, hid, topk):
    wa = single_columns(width)
    rows = tok // SLICES
    kind = jnp.bfloat16
    return [
        pltpu.VMEM((tok, width), kind),
        pltpu.VMEM((topk, tok), jnp.int32),
        pltpu.VMEM((topk, tok), kind),
        pltpu.VMEM((PLANES, 2, COLUMNS, 16, LANES), kind),
        pltpu.VMEM((PLANES, SLICES, 4 * rows, width), kind),
        pltpu.VMEM((width, hid), kind),
        pltpu.VMEM((width, hid), kind),
        pltpu.VMEM((hid, width), kind),
        pltpu.VMEM((PLANES, SLICES, 2 * rows, width), kind),
        pltpu.VMEM((2, 2 * rows, width), kind),
        pltpu.VMEM((2, 2 * rows, width), jnp.float32),
        pltpu.VMEM((2, PLANES - 1, SLICES, rows, max(wa)), kind),
        pltpu.VMEM((2, PLANES - 1, SLICES, 2 * rows, width - min(wa)), kind),
        pltpu.VMEM((PLANES, SLICES, rows, max(wa)), kind),
        pltpu.VMEM((SLICES, rows, width - min(wa)), kind),
    ]


def by_trees(tokens, gate_ids, gate_values, w_gate, w_up, w_down):
    tok, width = tokens.shape
    anywhere = pl.BlockSpec(memory_space=pl.ANY)

    def dma(*shape):
        return pltpu.SemaphoreType.DMA(shape)

    each = (PLANES, SLICES)
    return pl.pallas_call(
        tree_kernel,
        out_shape=jax.ShapeDtypeStruct((tok, width), jnp.bfloat16),
        in_specs=[anywhere] * 6,
        out_specs=anywhere,
        scratch_shapes=[
            *buffers(tok, width, w_gate.shape[2], gate_ids.shape[1]),
            dma(SLICES, PIECES + 1), dma(2), dma(3), dma(SLICES),
            dma(2, *each, PIECES), dma(*each, PIECES), dma(2, *each, 2), dma(*each, 2),
            dma(*each, PIECES), dma(*each, PIECES), dma(SLICES), dma(SLICES),
            dma(1), dma(1), dma(2, PLANES), dma(PLANES), dma(PLANES), dma(PLANES),
            dma(*each, 2), dma(*each, 2), dma(2), dma(*each),
            dma(*each, PIECES), dma(2, *each, PIECES), dma(*each, 2), dma(2, *each, 2),
            dma(*each, PIECES), dma(*each, PIECES), dma(SLICES), dma(SLICES),
        ],
        compiler_params=pltpu.CompilerParams(
            collective_id=0, has_side_effects=True, vmem_limit_bytes=VMEM_LIMIT
        ),
    )(tokens, gate_ids.T, gate_values.T, w_gate[0], w_up[0], w_down[0])


def by_collectives(tokens, gate_ids, gate_values, w_gate, w_up, w_down):
    n = lax.axis_size("node")
    every = ("node", "local")
    weights = lax.all_gather(expert_weights(gate_ids, gate_values, n), every, axis=0, tiled=True)
    rows = lax.all_gather(tokens, every, axis=0, tiled=True)
    mine = (jnp.arange(n, dtype=jnp.int32) == lax.axis_index("node"))[None, :]
    scale = jnp.sum(jnp.where(mine, weights.astype(jnp.float32), 0.0), axis=1, keepdims=True)
    gate_act = jnp.dot(rows, w_gate[0], preferred_element_type=jnp.float32)
    up_act = jnp.dot(rows, w_up[0], preferred_element_type=jnp.float32)
    hidden = (jax.nn.silu(gate_act) * up_act).astype(jnp.bfloat16)
    partial_value = jnp.dot(hidden, w_down[0], preferred_element_type=jnp.float32) * scale
    return lax.psum_scatter(
        partial_value.astype(jnp.bfloat16), every, scatter_dimension=0, tiled=True
    )


def trees_fit(n, tok, width, hid, topk):
    if n != PLANES * COLUMNS or lax.axis_size("local") != 2 or tok % (16 * SLICES) or width % LANES:
        return False
    if width < 2 * LANES or tok > LANES or n > 16:
        return False
    size = 2**21
    for ref in buffers(tok, width, hid, topk):
        size += ref.inner_aval.size * ref.inner_aval.dtype.itemsize
    return size < VMEM_LIMIT


def per_device(tokens, gate_ids, gate_values, w_gate, w_up, w_down):
    n = lax.axis_size("node")
    args = (tokens, gate_ids, gate_values, w_gate, w_up, w_down)
    if trees_fit(n, *tokens.shape, w_gate.shape[2], gate_ids.shape[1]):
        return by_trees(*args)
    return by_collectives(*args)


def solution(mesh):
    return jax.shard_map(
        per_device,
        mesh=mesh,
        in_specs=(
            P(("rep", "node", "local"), None),
            P(("rep", "node", "local"), None),
            P(("rep", "node", "local"), None),
            P("node", None, "local"),
            P("node", None, "local"),
            P("node", "local", None),
        ),
        out_specs=P(("rep", "node", "local"), None),
        check_vma=False,
    )
```
